256 devices in a mesh: lead: 8 (over x, core), space: 32 (over z, y).
Axes of the slice: x: 4, y: 4, z: 8, core: 2. Of those that a mesh axis runs over, the one named last changes fastest.
Arguments:
- states: bfloat16 [8, 8, 64, 128, 768], P('lead', None, 'space'), may hold values from -6 to 6
- filter_in: bfloat16 [2, 8, 96, 96], replicated, may hold values from -0.4375 to 0.4375
- filter_out: bfloat16 [2, 8, 96, 96], replicated, may hold values from -0.21875 to 0.21875
- filter_bias: float32 [2, 768], replicated, may hold values from -6 to 6
- decoder: bfloat16 [768, 128], replicated, may hold values from -0.5 to 0.5
- obs_value: float32 [8, 8, 131072], P('lead', None, 'space'), may hold values from -6 to 6
- obs_weight: float32 [8, 131072], P('lead', 'space'), may hold values from 0.5 to 2
- obs_index: int32 [8, 131072], P('lead', 'space'), may hold values from 0 to 32767
- block_dest: int32 [8, 1024], P('lead', 'space'), may hold values from 0 to 31, as said below
- block_count: int32 [8, 1024], P('lead', 'space'), may hold values from 96 to 128
Outputs:
- adjoint_fields: bfloat16 [8, 8, 64, 128, 768], P('lead', None, 'space')
The draws below stay inside these ranges and needn't reach their ends.
Inputs may be any that keep to these rules, and one draw needn't show every extreme that they name: `block_dest`: at most 2 blocks of one owner in one section name the same tile, and in each section one tile is named by exactly 2 blocks of every owner.
All inputs are finite; a program needn't handle non-finite values.
Results may differ from the reference program's by a relative error of at most 0.017.
Values may be sent and summed in bfloat16 or wider, within the bound.
No kernel may reach another device: no remote copies, remote signals or barrier semaphores. Data moves between devices by JAX's collectives and lax.ppermute only.
A program may use at most 128 MiB of HBM per device.

```python
import math
import jax
import jax.numpy as jnp
from jax import lax

NLAT = 64
NLON = 128
C = 768
BS = 96
NVAR = 128
OBS_BLK = 128
BLK_DEV = 32
MEMBERS = 8
CAP = 2
SECTIONS = 8
NB = 8
CELLS_DEV = 256
OBS_ROWS = 131072
N_SPACE = 32


def draw_block_dest(key, part):
    tiles = N_SPACE
    crowded = jax.random.randint(jax.random.fold_in(key, 11), (SECTIONS, 1, 1), 0, tiles)
    offset = jax.random.randint(jax.random.fold_in(key, 12), (SECTIONS, tiles, 1), 0, tiles - 1)
    position = jnp.arange(BLK_DEV, dtype=jnp.int32)[None, None, :]
    others = position - CAP
    spread = (crowded + 1 + (offset + others) % (tiles - 1)) % tiles
    target = jnp.where(position < CAP, crowded, spread)
    scores = jax.random.randint(jax.random.fold_in(key, 13), (SECTIONS, tiles, BLK_DEV), 0, 1 << 20) * BLK_DEV + position
    shuffle = jnp.argsort(scores, axis=2)
    target = jnp.take_along_axis(target, shuffle, axis=2)
    return target.reshape(SECTIONS, tiles * BLK_DEV).astype(jnp.int32)


def plant(array, stream_key, low, largest):
    extent = array.shape
    spot = [jax.random.randint(jax.random.fold_in(stream_key, axis), (), 0, extent[axis]) for axis in range(len(extent))]
    array = array.at[tuple(spot)].set(low)
    longest = extent.index(max(extent))
    spot[longest] = (spot[longest] + 1) % extent[longest]
    return array.at[tuple(spot)].set(largest)


def block_scale(stream_key, extent, shards, least, top_value):
    gain = 1.0
    for dim, parts in shards:
        heights = jax.random.uniform(jax.random.fold_in(jax.random.fold_in(stream_key, 6), dim), (parts,), jnp.float32, least / len(shards), top_value / len(shards))
        gain = gain * jnp.repeat(jnp.exp(heights), extent[dim] // parts).reshape((-1,) + (1,) * (len(extent) - 1 - dim))
    return gain


def gaussian(stream_key, extent, scale, most, pieces=(), kind=jnp.bfloat16):
    result = scale * jax.random.normal(stream_key, extent, jnp.float32)
    if pieces:
        result = result * block_scale(stream_key, extent, pieces, -0.22, 0.18)
    return jnp.clip(result, -most, most).astype(kind)


def setup_inputs(seed: int = 0) -> dict:
    streams_of = jax.random.split(jax.random.key(seed), 11)
    states = gaussian(streams_of[0], (SECTIONS, MEMBERS, NLAT, NLON, C), 1.0, 6.0, ((0, 8), (2, 32)))
    filter_in = gaussian(streams_of[1], (2, NB, BS, BS), (2 * BS) ** -0.5, 0.4375)
    filter_out = gaussian(streams_of[2], (2, NB, BS, BS), (8 * BS) ** -0.5, 0.21875)
    filter_bias = gaussian(streams_of[3], (2, C), 1.0, 6.0, (), jnp.float32)
    decoder = gaussian(streams_of[4], (C, NVAR), NVAR ** -0.5, 0.5)
    obs_value = gaussian(streams_of[5], (SECTIONS, MEMBERS, OBS_ROWS), 1.0, 6.0, ((0, 8), (2, 32)), jnp.float32)
    obs_weight = jnp.clip(jnp.exp(math.log(2.0) - 1.3862944 * jax.random.uniform(streams_of[6], (SECTIONS, OBS_ROWS), jnp.float32) ** block_scale(streams_of[6], (SECTIONS, OBS_ROWS), ((0, 8), (1, 32)), -0.2, 0.2)), 0.5, 2.0)
    obs_index = plant(jax.random.randint(streams_of[7], (SECTIONS, OBS_ROWS), 0, CELLS_DEV * NVAR), jax.random.fold_in(streams_of[7], 1), 0, (CELLS_DEV * NVAR) - 1).astype(jnp.int32)
    block_dest = draw_block_dest(jax.random.fold_in(streams_of[10], 71), 0)
    block_count = plant(jax.random.randint(streams_of[9], (SECTIONS, N_SPACE * BLK_DEV), 3 * OBS_BLK // 4, OBS_BLK + 1), jax.random.fold_in(streams_of[9], 1), 3 * OBS_BLK // 4, OBS_BLK).astype(jnp.int32)
    return {"states": states, "filter_in": filter_in, "filter_out": filter_out, "filter_bias": filter_bias, "decoder": decoder, "obs_value": obs_value, "obs_weight": obs_weight, "obs_index": obs_index, "block_dest": block_dest, "block_count": block_count}


root_scale = math.sqrt(2.0 / math.pi)
cubic_term = 0.044715

def gelu_slope(values):
    argument = root_scale * (values + cubic_term * values * values * values)
    tangent = jnp.tanh(argument)
    return 0.5 * (1.0 + tangent) + 0.5 * values * (1.0 - tangent * tangent) * root_scale * (1.0 + 3.0 * cubic_term * values * values)

def wave_table(row_count, col_count, length):
    row_index = lax.broadcasted_iota(jnp.int32, (row_count, col_count), 0)
    col_index = lax.broadcasted_iota(jnp.int32, (row_count, col_count), 1)
    angles = (row_index * col_index % length).astype(jnp.float32) * (2.0 * math.pi / length)
    return (jnp.cos(angles), jnp.sin(angles))

def make_tables(lon_len, lat_len):
    mode_count = lon_len // 2
    lon_scale = 1.0 / math.sqrt(lon_len)
    lat_scale = 1.0 / math.sqrt(lat_len)
    cos_fore, sin_fore = wave_table(lon_len, mode_count, lon_len)
    cos_back, sin_back = wave_table(mode_count, lon_len, lon_len)
    factor = jnp.where(lax.broadcasted_iota(jnp.int32, (mode_count, 1), 0) == 0, 1.0, 2.0).astype(jnp.float32)
    cos_lat, sin_lat = wave_table(lat_len, lat_len, lat_len)
    lon_cos = (cos_fore * lon_scale).astype(jnp.bfloat16)
    lon_sin = (-sin_fore * lon_scale).astype(jnp.bfloat16)
    back_cos = (factor * cos_back * lon_scale).astype(jnp.bfloat16)
    back_sin = (-factor * sin_back * lon_scale).astype(jnp.bfloat16)
    lat_cos = (cos_lat * lat_scale).astype(jnp.bfloat16)
    lat_sin = (sin_lat * lat_scale).astype(jnp.bfloat16)
    return (lon_cos, lon_sin, back_cos, back_sin, lat_cos, lat_sin)

def contract(pattern, left_op, right_op):
    return jnp.einsum(pattern, left_op.astype(jnp.float32), right_op.astype(jnp.float32), precision=lax.Precision.HIGHEST)

def block_mix(operand, matrix):
    split_view = operand.reshape(operand.shape[:-1] + (matrix.shape[0], matrix.shape[1]))
    return contract('...ni,nio->...no', split_view, matrix).reshape(operand.shape)

def block_mix_t(operand, matrix):
    split_view = operand.reshape(operand.shape[:-1] + (matrix.shape[0], matrix.shape[2]))
    return contract('...no,nio->...ni', split_view, matrix).reshape(operand.shape)

def section_modes(fields, tables, filter_in, filter_bias):
    lon_cos, lon_sin, lat_cos, lat_sin = (tables[0], tables[1], tables[4], tables[5])
    spec_re = contract('mfnc,nk->mfkc', fields, lon_cos).astype(jnp.bfloat16)
    spec_im = contract('mfnc,nk->mfkc', fields, lon_sin).astype(jnp.bfloat16)
    mode_re = (contract('pf,mfkc->mpkc', lat_cos, spec_re) + contract('pf,mfkc->mpkc', lat_sin, spec_im)).astype(jnp.bfloat16)
    mode_im = (contract('pf,mfkc->mpkc', lat_cos, spec_im) - contract('pf,mfkc->mpkc', lat_sin, spec_re)).astype(jnp.bfloat16)
    pre_re = block_mix(mode_re, filter_in[0]) - block_mix(mode_im, filter_in[1]) + filter_bias[0]
    pre_im = block_mix(mode_re, filter_in[1]) + block_mix(mode_im, filter_in[0]) + filter_bias[1]
    return (pre_re, pre_im)

def section_adjoint(incoming, pre_re, pre_im, tables, filter_in, filter_out):
    lon_cos, lon_sin, back_cos, back_sin, lat_cos, lat_sin = tables
    back_re = contract('mfnc,kn->mfkc', incoming, back_cos).astype(jnp.bfloat16)
    back_im = contract('mfnc,kn->mfkc', incoming, back_sin).astype(jnp.bfloat16)
    out_re = (contract('fp,mfkc->mpkc', lat_cos, back_re) + contract('fp,mfkc->mpkc', lat_sin, back_im)).astype(jnp.bfloat16)
    out_im = (contract('fp,mfkc->mpkc', lat_cos, back_im) - contract('fp,mfkc->mpkc', lat_sin, back_re)).astype(jnp.bfloat16)
    hid_re = block_mix_t(out_re, filter_out[0]) + block_mix_t(out_im, filter_out[1])
    hid_im = block_mix_t(out_im, filter_out[0]) - block_mix_t(out_re, filter_out[1])
    act_re = (hid_re * gelu_slope(pre_re)).astype(jnp.bfloat16)
    act_im = (hid_im * gelu_slope(pre_im)).astype(jnp.bfloat16)
    grad_re = (block_mix_t(act_re, filter_in[0]) + block_mix_t(act_im, filter_in[1])).astype(jnp.bfloat16)
    grad_im = (block_mix_t(act_im, filter_in[0]) - block_mix_t(act_re, filter_in[1])).astype(jnp.bfloat16)
    lat_re = (contract('pf,mpkc->mfkc', lat_cos, grad_re) - contract('pf,mpkc->mfkc', lat_sin, grad_im)).astype(jnp.bfloat16)
    lat_im = (contract('pf,mpkc->mfkc', lat_sin, grad_re) + contract('pf,mpkc->mfkc', lat_cos, grad_im)).astype(jnp.bfloat16)
    return contract('mfkc,nk->mfnc', lat_re, lon_cos) + contract('mfkc,nk->mfnc', lat_im, lon_sin)

def section_forcing(fields, decoder, values, weights, obs_cells, targets, counts):
    member_count, lat_len, lon_len = (fields.shape[0], fields.shape[1], fields.shape[2])
    levels = decoder.shape[1]
    decoded = contract('mfnc,cv->mfnv', fields, decoder).reshape(member_count, lat_len * lon_len * levels)
    row_total = obs_cells.shape[0]
    block_len = row_total // targets.shape[0]
    row_dest = jnp.repeat(targets, block_len, total_repeat_length=row_total)
    row_count = jnp.repeat(counts, block_len, total_repeat_length=row_total)
    within = jnp.arange(row_total, dtype=jnp.int32) % block_len
    weight_live = jnp.where(within < row_count, weights, 0.0)
    position = row_dest * (CELLS_DEV * levels) + obs_cells
    innovation = weight_live[None, :] * (decoded[:, position] - values)
    spread_sum = jnp.zeros_like(decoded).at[:, position].add(innovation).astype(jnp.bfloat16)
    return contract('mfnv,cv->mfnc', spread_sum.reshape(member_count, lat_len, lon_len, levels), decoder)

def reference(states, filter_in, filter_out, filter_bias, decoder, obs_value, obs_weight, obs_index, block_dest, block_count):
    tables = make_tables(states.shape[3], states.shape[2])
    incoming = jnp.zeros(states.shape[1:], jnp.bfloat16)
    results = []
    for section in range(SECTIONS - 1, -1, -1):
        fields = states[section]
        pre_re, pre_im = section_modes(fields, tables, filter_in, filter_bias)
        forcing = section_forcing(fields, decoder, obs_value[section], obs_weight[section], obs_index[section], block_dest[section], block_count[section])
        lift = section_adjoint(incoming, pre_re, pre_im, tables, filter_in, filter_out)
        incoming = (incoming.astype(jnp.float32) + lift + forcing).astype(jnp.bfloat16)
        results.append(incoming)
    return jnp.stack(results[::-1], 0)
```

```python
import math

import jax
import jax.numpy as jnp
import numpy as np
from jax import lax
from jax.experimental import pallas as pl
from jax.experimental.pallas import tpu as pltpu
from jax.sharding import PartitionSpec as P

OBS_BLK = 128
EVERY = ("lead", "space")

root_scale = math.sqrt(2.0 / math.pi)
cubic_term = 0.044715


def gelu_slope(values):
    square = values * values
    tangent = jnp.tanh(values * (root_scale + (root_scale * cubic_term) * square))
    bend = values * ((0.5 * root_scale) + (1.5 * root_scale * cubic_term) * square)
    return 0.5 + 0.5 * tangent + bend * (1.0 - tangent * tangent)


def waves(rows, cols, length):
    angle = (np.outer(np.arange(rows), np.arange(cols)) % length) * (2.0 * math.pi / length)
    return np.cos(angle), np.sin(angle)


def make_matrices(tiles, lat_local, lon_len):
    lat_len, modes = tiles * lat_local, lon_len // 2
    pair = modes // tiles
    cos, sin = waves(modes, lon_len, lon_len)
    scale = 1.0 / math.sqrt(lon_len)
    gain = np.where(np.arange(modes) == 0, 1.0, 2.0)[:, None]
    nyquist = np.cos(math.pi * np.arange(lon_len)) * scale

    def zonal(factor, full):
        parts = np.stack([factor * cos * scale, -factor * sin * scale])
        parts[1, 0] = nyquist if full else 0.0
        parts = parts.reshape(2, tiles, pair, lon_len).transpose(1, 0, 2, 3)
        out = np.zeros((tiles, lat_local, 2, pair, lat_local, lon_len))
        for f in range(lat_local):
            out[:, f, :, :, f] = parts
        return out.reshape(tiles * lat_local * 2 * pair, lat_local * lon_len)

    lat_cos, lat_sin = (t / math.sqrt(lat_len) for t in waves(lat_len, lat_len, lat_len))
    merid = np.zeros((2, pair, lat_len, lat_len, 2, pair))
    for k in range(pair):
        merid[0, k, :, :, 0, k] = lat_cos
        merid[0, k, :, :, 1, k] = lat_sin
        merid[1, k, :, :, 0, k] = -lat_sin
        merid[1, k, :, :, 1, k] = lat_cos
    merid = merid.reshape(2 * pair * lat_len, lat_len * 2 * pair)
    herm = np.zeros((2, pair, lat_len, 2, pair, lat_len))
    flip = (-np.arange(lat_len)) % lat_len
    for k in range(pair):
        for part in range(2):
            for p in range(lat_len):
                if k == 0:
                    herm[part, k, p, part, k, p] += 0.5
                    herm[part, k, p, part, k, flip[p]] += 0.5 if part == 0 else -0.5
                else:
                    herm[part, k, p, part, k, p] = 1.0
    herm = herm.reshape(2 * pair * lat_len, 2 * pair * lat_len)
    return {
        "state": zonal(1.0, False).astype(np.float32),
        "force": zonal(gain, True).astype(np.float32),
        "back": zonal(1.0, True).T.astype(np.float32),
        "merid": merid.astype(np.float32),
        "merid_t": merid.T.astype(np.float32),
        "herm": herm.astype(np.float32),
    }


def dot(a, b):
    return lax.dot_general(a, b, (((1,), (0,)), ((), ())), preferred_element_type=jnp.float32)


def dot_nt(a, b):
    return lax.dot_general(a, b, (((1,), (1,)), ((), ())), preferred_element_type=jnp.float32)


def mix_rows(matrix, array):
    batch, rows, cols = array.shape
    out_rows = matrix.shape[0]

    def body(m_ref, x_ref, o_ref):
        o_ref[0] = dot(m_ref[...], x_ref[0]).astype(o_ref.dtype)

    return pl.pallas_call(
        body,
        out_shape=jax.ShapeDtypeStruct((batch, out_rows, cols), jnp.bfloat16),
        grid=(batch,),
        in_specs=[
            pl.BlockSpec((out_rows, rows), lambda b: (0, 0)),
            pl.BlockSpec((1, rows, cols), lambda b: (b, 0, 0)),
        ],
        out_specs=pl.BlockSpec((1, out_rows, cols), lambda b: (b, 0, 0)),
        name="mix_rows",
    )(matrix, array)


def pack_outbox(obs_value, obs_weight, obs_index, block_dest, block_count, tiles):
    members, rows = obs_value.shape
    blocks = rows // OBS_BLK

    def body(dest_ref, count_ref, value_ref, weight_ref, index_ref, o_ref, seen_ref):
        o_ref[...] = jnp.zeros_like(o_ref)
        lane = lax.broadcasted_iota(jnp.int32, (1, OBS_BLK), 1)
        for t in range(tiles):
            seen_ref[t] = 0
        for b in range(blocks):
            tile = dest_ref[b]
            rank = seen_ref[tile]
            seen_ref[tile] = rank + 1
            span = slice(b * OBS_BLK, (b + 1) * OBS_BLK)
            weight = jnp.where(lane < count_ref[b], weight_ref[:, span], 0.0)
            o_ref[tile, pl.ds(pl.multiple_of(rank * members, members), members), :] = (
                value_ref[:, span] * weight
            )
            o_ref[tile, pl.ds(2 * members + rank, 1), :] = weight
            o_ref[tile, pl.ds(2 * members + 2 + rank, 1), :] = index_ref[:, span].astype(jnp.float32)

    smem = pl.BlockSpec(memory_space=pltpu.SMEM)
    vmem = pl.BlockSpec(memory_space=pltpu.VMEM)
    return pl.pallas_call(
        body,
        out_shape=jax.ShapeDtypeStruct((tiles, 2 * members + 8, OBS_BLK), jnp.float32),
        in_specs=[smem, smem, vmem, vmem, vmem],
        out_specs=vmem,
        scratch_shapes=[pltpu.SMEM((tiles,), jnp.int32)],
        name="pack_outbox",
    )(block_dest, block_count, obs_value, obs_weight, obs_index)


def level_spectra(received, decoded, matrix):
    sources, rows, lanes = received.shape
    members, cells, levels = decoded.shape
    group = 4
    wide = 2 * lanes
    span = group * wide

    def body(got_ref, dec_ref, mat_ref, o_ref, cell_ref, val_ref, acc_ref):
        acc_ref[...] = jnp.zeros_like(acc_ref)
        cell_iota = lax.broadcasted_iota(jnp.int32, (cells, wide), 0)
        level_iota = lax.broadcasted_iota(jnp.int32, (levels, wide), 0)

        def one_group(g, carry):
            for u in range(group):
                got = got_ref[g * group + u]
                index = jnp.concatenate(
                    [got[2 * members + 2 : 2 * members + 3], got[2 * members + 3 : 2 * members + 4]], axis=1
                ).astype(jnp.int32)
                cell, level = index // levels, index % levels
                first, second = u * wide, span + u * wide
                hot_cell = (cell_iota == cell).astype(jnp.bfloat16)
                cell_ref[:, first : first + wide] = hot_cell
                cell_ref[:, second : second + wide] = hot_cell
                hot_level = (level_iota == level).astype(jnp.bfloat16)
                weight = jnp.concatenate(
                    [got[2 * members : 2 * members + 1], got[2 * members + 1 : 2 * members + 2]], axis=1
                )
                value = jnp.concatenate([got[:members], got[members : 2 * members]], axis=1)
                full = jnp.concatenate([weight, value], axis=0)
                high = full.astype(jnp.bfloat16)
                low = (full - high.astype(jnp.float32)).astype(jnp.bfloat16)
                for q in range(members + 1):
                    at = slice(q * levels, (q + 1) * levels)
                    val_ref[at, first : first + wide] = hot_level * high[q : q + 1]
                    val_ref[at, second : second + wide] = hot_level * low[q : q + 1]
            acc_ref[...] += dot_nt(cell_ref[...], val_ref[...])
            return carry

        lax.fori_loop(0, sources // group, one_group, 0)
        weights = acc_ref[:, :levels]
        for q in range(members):
            forcing = weights * dec_ref[q] - acc_ref[:, (q + 1) * levels : (q + 2) * levels]
            o_ref[q] = dot(mat_ref[...], forcing.astype(jnp.bfloat16)).astype(jnp.bfloat16)

    vmem = pl.BlockSpec(memory_space=pltpu.VMEM)
    return pl.pallas_call(
        body,
        out_shape=jax.ShapeDtypeStruct((members, matrix.shape[0], levels), jnp.bfloat16),
        in_specs=[vmem, vmem, vmem],
        out_specs=vmem,
        scratch_shapes=[
            pltpu.VMEM((cells, 2 * span), jnp.bfloat16),
            pltpu.VMEM(((members + 1) * levels, 2 * span), jnp.bfloat16),
            pltpu.VMEM((cells, (members + 1) * levels), jnp.float32),
        ],
        name="level_spectra",
    )(received, decoded, matrix)


def sweep(spectra, level_spec, merid, merid_t, herm, mats, bias, decoder_t):
    sections, rows, cols = spectra.shape
    levels = level_spec.shape[2]
    chunks, width = mats.shape[1], mats.shape[2]
    half = rows // 2

    def body(x_ref, f_ref, d_ref, dt_ref, h_ref, w_ref, b_ref, dec_ref, o_ref, z_ref):
        @pl.when(pl.program_id(0) == 0)
        def _():
            z_ref[...] = jnp.zeros_like(z_ref)

        forced = dot(d_ref[...], f_ref[0]).astype(jnp.bfloat16)
        for c in range(chunks):
            at = slice(c * width, (c + 1) * width)
            mode = dot(d_ref[...], x_ref[0, :, at]).astype(jnp.bfloat16)
            by_re, by_im = dot(mode, w_ref[0, c]), dot(mode, w_ref[1, c])
            slope_re = gelu_slope(by_re[:half] - by_im[half:] + b_ref[0:1, at])
            slope_im = gelu_slope(by_im[:half] + by_re[half:] + b_ref[1:2, at])
            carry = z_ref[:, at]
            out = dot(h_ref[...], carry.astype(jnp.bfloat16)).astype(jnp.bfloat16)
            by_re, by_im = dot(out, w_ref[2, c]), dot(out, w_ref[3, c])
            act_re = ((by_re[:half] + by_im[half:]) * slope_re).astype(jnp.bfloat16)
            act_im = ((by_re[half:] - by_im[:half]) * slope_im).astype(jnp.bfloat16)
            act = jnp.concatenate([act_re, act_im], axis=0)
            by_re, by_im = dot(act, w_ref[4, c]), dot(act, w_ref[5, c])
            grad = jnp.concatenate(
                [
                    (by_re[:half] + by_im[half:]).astype(jnp.bfloat16),
                    (by_re[half:] - by_im[:half]).astype(jnp.bfloat16),
                ],
                axis=0,
            )
            carry = carry + dot(h_ref[...], grad) + dot(forced, dec_ref[:, at])
            z_ref[:, at] = carry
            o_ref[0, :, at] = dot(dt_ref[...], carry.astype(jnp.bfloat16)).astype(jnp.bfloat16)

    def whole(shape):
        return pl.BlockSpec(shape, lambda t: (0,) * len(shape))

    def turn(shape):
        return pl.BlockSpec(shape, lambda t: (sections - 1 - t, 0, 0))

    return pl.pallas_call(
        body,
        out_shape=jax.ShapeDtypeStruct(spectra.shape, jnp.bfloat16),
        grid=(sections,),
        in_specs=[
            turn((1, rows, cols)),
            turn((1, rows, levels)),
            whole(merid.shape),
            whole(merid_t.shape),
            whole(herm.shape),
            whole(mats.shape),
            whole(bias.shape),
            whole(decoder_t.shape),
        ],
        out_specs=turn((1, rows, cols)),
        scratch_shapes=[pltpu.VMEM((rows, cols), jnp.float32)],
        name="sweep",
    )(spectra, level_spec, merid, merid_t, herm, mats, bias, decoder_t)


def block_diagonal(weights, chunks):
    pieces, blocks, size, _ = weights.shape
    per = blocks // chunks
    split = weights.reshape(pieces, chunks, per, size, 1, size)
    mask = jnp.eye(per, dtype=weights.dtype).reshape(1, 1, per, 1, per, 1)
    return (split * mask).reshape(pieces, chunks, per * size, per * size)


def swap(array, axis):
    batch, rows, cols = array.shape
    return lax.all_to_all(
        array.reshape(-1, 8, cols), axis, split_axis=0, concat_axis=0, tiled=True
    ).reshape(batch, rows, cols)


def shards(
    states,
    filter_in,
    filter_out,
    filter_bias,
    decoder,
    obs_value,
    obs_weight,
    obs_index,
    block_dest,
    block_count,
):
    member_count, lat_local, lon_len, channels = states.shape[1:]
    tiles = lax.axis_size("space")
    tables = {
        name: jnp.asarray(table, jnp.bfloat16)
        for name, table in make_matrices(tiles, lat_local, lon_len).items()
    }
    fields = states.reshape(member_count, lat_local * lon_len, channels)
    outbox = pack_outbox(obs_value[0], obs_weight, obs_index, block_dest[0], block_count[0], tiles)
    received = lax.all_to_all(outbox, "space", split_axis=0, concat_axis=0, tiled=True)
    spectra = swap(mix_rows(tables["state"], fields), EVERY)
    decoded = jnp.einsum("mnc,cv->mnv", fields, decoder, preferred_element_type=jnp.float32)
    levels = swap(level_spectra(received, decoded, tables["force"]), EVERY)
    chunks = 2
    weights = jnp.concatenate(
        [filter_in, jnp.swapaxes(filter_out, 2, 3), jnp.swapaxes(filter_in, 2, 3)], axis=0
    )
    mats = block_diagonal(weights, chunks)
    herm = jnp.where(
        lax.axis_index("space") == 0, tables["herm"], jnp.eye(tables["herm"].shape[0], dtype=jnp.bfloat16)
    )
    swept = sweep(
        spectra, levels, tables["merid"], tables["merid_t"], herm, mats, filter_bias, decoder.T
    )
    result = mix_rows(tables["back"], swap(swept, EVERY))
    return result.reshape(1, member_count, lat_local, lon_len, channels)


def solution(mesh):
    placed = (
        P("lead", None, "space", None, None),
        P(),
        P(),
        P(),
        P(),
        P("lead", None, "space"),
        P("lead", "space"),
        P("lead", "space"),
        P("lead", "space"),
        P("lead", "space"),
    )
    return jax.shard_map(
        shards,
        mesh=mesh,
        in_specs=placed,
        out_specs=P("lead", None, "space", None, None),
        check_vma=False,
    )
```

```python
import math

import jax
import jax.numpy as jnp
import numpy as np
from jax import lax
from jax.experimental import pallas as pl
from jax.experimental.pallas import tpu as pltpu
from jax.sharding import PartitionSpec as P

OBS_BLK = 128
EVERY = ("lead", "space")

root_scale = math.sqrt(2.0 / math.pi)
cubic_term = 0.044715


def gelu_slope(values):
    square = values * values
    tangent = jnp.tanh(values * (root_scale + (root_scale * cubic_term) * square))
    bend = values * ((0.5 * root_scale) + (1.5 * root_scale * cubic_term) * square)
    return 0.5 + 0.5 * tangent + bend * (1.0 - tangent * tangent)


def waves(rows, cols, length):
    angle = (np.outer(np.arange(rows), np.arange(cols)) % length) * (2.0 * math.pi / length)
    return np.cos(angle), np.sin(angle)


def make_matrices(tiles, lat_local, lon_len):
    lat_len, modes = tiles * lat_local, lon_len // 2
    pair = modes // tiles
    cos, sin = waves(modes, lon_len, lon_len)
    scale = 1.0 / math.sqrt(lon_len)
    gain = np.where(np.arange(modes) == 0, 1.0, 2.0)[:, None]
    nyquist = np.cos(math.pi * np.arange(lon_len)) * scale

    def zonal(factor, full):
        parts = np.stack([factor * cos * scale, -factor * sin * scale])
        parts[1, 0] = nyquist if full else 0.0
        parts = parts.reshape(2, tiles, pair, lon_len).transpose(1, 0, 2, 3)
        out = np.zeros((tiles, lat_local, 2, pair, lat_local, lon_len))
        for f in range(lat_local):
            out[:, f, :, :, f] = parts
        return out.reshape(tiles * lat_local * 2 * pair, lat_local * lon_len)

    lat_cos, lat_sin = (t / math.sqrt(lat_len) for t in waves(lat_len, lat_len, lat_len))
    merid = np.zeros((2, pair, lat_len, lat_len, 2, pair))
    for k in range(pair):
        merid[0, k, :, :, 0, k] = lat_cos
        merid[0, k, :, :, 1, k] = lat_sin
        merid[1, k, :, :, 0, k] = -lat_sin
        merid[1, k, :, :, 1, k] = lat_cos
    merid = merid.reshape(2 * pair * lat_len, lat_len * 2 * pair)
    herm = np.zeros((2, pair, lat_len, 2, pair, lat_len))
    flip = (-np.arange(lat_len)) % lat_len
    for k in range(pair):
        for part in range(2):
            for p in range(lat_len):
                if k == 0:
                    herm[part, k, p, part, k, p] += 0.5
                    herm[part, k, p, part, k, flip[p]] += 0.5 if part == 0 else -0.5
                else:
                    herm[part, k, p, part, k, p] = 1.0
    herm = herm.reshape(2 * pair * lat_len, 2 * pair * lat_len)
    return {
        "state": zonal(1.0, False).astype(np.float32),
        "force": zonal(gain, True).astype(np.float32),
        "back": zonal(1.0, True).T.astype(np.float32),
        "merid": merid.astype(np.float32),
        "merid_t": merid.T.astype(np.float32),
        "herm": herm.astype(np.float32),
    }


def dot(a, b):
    return lax.dot_general(a, b, (((1,), (0,)), ((), ())), preferred_element_type=jnp.float32)


def dot_nt(a, b):
    return lax.dot_general(a, b, (((1,), (1,)), ((), ())), preferred_element_type=jnp.float32)


def cost(products, moved):
    return pl.CostEstimate(flops=2 * products, transcendentals=0, bytes_accessed=moved)


def mix_rows(matrix, array, per_step=2):
    batch, rows, cols = array.shape

    def body(m_ref, x_ref, o_ref):
        for u in range(per_step):
            o_ref[u] = dot(m_ref[...], x_ref[u]).astype(jnp.bfloat16)

    part = pl.BlockSpec((per_step, rows, cols), lambda b: (b, 0, 0))
    return pl.pallas_call(
        body,
        out_shape=jax.ShapeDtypeStruct(array.shape, jnp.bfloat16),
        grid=(batch // per_step,),
        in_specs=[pl.BlockSpec((rows, rows), lambda b: (0, 0)), part],
        out_specs=part,
        cost_estimate=cost(batch * rows * rows * cols, 4 * batch * rows * cols),
        name="mix_rows",
    )(matrix, array)


def dense_blocks(filter_in, filter_out, chunks):
    _, blocks, size, _ = filter_in.shape
    per = blocks // chunks
    width = per * size
    lift = np.tile(np.eye(size, dtype=np.float32), (per, 1))
    same = np.kron(np.eye(per, dtype=np.float32), np.ones((size, size), np.float32))

    def body(in_ref, out_ref, lift_ref, same_ref, f_ref, a_ref):
        same_block = same_ref[...]
        for c in range(chunks):
            for q in range(2):
                at = slice(q * width, (q + 1) * width)
                w_in = in_ref[q, c * per : (c + 1) * per].reshape(width, size)
                w_out = out_ref[q, c * per : (c + 1) * per].reshape(width, size)
                f_ref[0, c, at] = (dot_nt(w_in, lift_ref[...]) * same_block).astype(jnp.bfloat16)
                a_ref[0, c, at] = (dot_nt(lift_ref[...], w_out) * same_block).astype(jnp.bfloat16)
                a_ref[1, c, at] = (dot_nt(lift_ref[...], w_in) * same_block).astype(jnp.bfloat16)

    vmem = pl.BlockSpec(memory_space=pltpu.VMEM)
    return pl.pallas_call(
        body,
        out_shape=(
            jax.ShapeDtypeStruct((1, chunks, 2 * width, width), jnp.bfloat16),
            jax.ShapeDtypeStruct((2, chunks, 2 * width, width), jnp.bfloat16),
        ),
        in_specs=[vmem] * 4,
        out_specs=(vmem, vmem),
        cost_estimate=cost(12 * width * width * size, 12 * width * width),
        name="dense_blocks",
    )(filter_in, filter_out, jnp.asarray(lift, jnp.bfloat16), jnp.asarray(same, jnp.float32))


def pack_outbox(obs_value, obs_weight, obs_index, block_dest, block_count, here, near, far):
    members, rows = obs_value.shape
    blocks = rows // OBS_BLK
    height = 2 * members + 8

    def body(here_ref, dest_ref, count_ref, value_ref, weight_ref, index_ref, *rest):
        o_refs, box_ref, seen_ref = rest[:near], rest[near], rest[near + 1]
        box_ref[...] = jnp.zeros_like(box_ref)
        lane = lax.broadcasted_iota(jnp.int32, (1, OBS_BLK), 1)
        my_far, my_near = here_ref[0] // near, here_ref[0] % near
        for t in range(near * far):
            seen_ref[t] = 0
        for b in range(blocks):
            tile = dest_ref[b]
            slot = (tile % near + near - my_near) % near * far + (tile // near + far - my_far) % far
            rank = seen_ref[tile]
            seen_ref[tile] = rank + 1
            span = slice(b * OBS_BLK, (b + 1) * OBS_BLK)
            weight = jnp.where(lane < count_ref[b], weight_ref[:, span], 0.0)
            box_ref[slot, pl.ds(pl.multiple_of(rank * members, members), members), :] = (
                value_ref[:, span] * weight
            )
            box_ref[slot, pl.ds(2 * members + rank, 1), :] = weight
            box_ref[slot, pl.ds(2 * members + 2 + rank, 1), :] = index_ref[:, span].astype(jnp.float32)
        for r in range(near):
            o_refs[r][...] = box_ref[r * far : (r + 1) * far]

    smem = pl.BlockSpec(memory_space=pltpu.SMEM)
    vmem = pl.BlockSpec(memory_space=pltpu.VMEM)
    return pl.pallas_call(
        body,
        out_shape=[jax.ShapeDtypeStruct((far, height, OBS_BLK), jnp.float32)] * near,
        in_specs=[smem, smem, smem, vmem, vmem, vmem],
        out_specs=[vmem] * near,
        scratch_shapes=[
            pltpu.VMEM((near * far, height, OBS_BLK), jnp.float32),
            pltpu.SMEM((near * far,), jnp.int32),
        ],
        name="pack_outbox",
    )(here, block_dest, block_count, obs_value, obs_weight, obs_index)


def regroup(arrays):
    near, far = len(arrays), arrays[0].shape[0]
    rest = arrays[0].shape[1:]

    def body(*refs):
        for q in range(far):
            for r in range(near):
                refs[near + q][r] = refs[r][q]

    vmem = pl.BlockSpec(memory_space=pltpu.VMEM)
    return pl.pallas_call(
        body,
        out_shape=[jax.ShapeDtypeStruct((near,) + rest, arrays[0].dtype)] * far,
        in_specs=[vmem] * near,
        out_specs=[vmem] * far,
        name="regroup",
    )(*arrays)


def route(arrays, near, far):
    def shift(array, by_near, by_far):
        perm = [
            (z * near + y, (z + by_far) % far * near + (y + by_near) % near)
            for z in range(far)
            for y in range(near)
        ]
        return lax.ppermute(array, "space", perm)

    arrays = [arrays[0]] + [shift(arrays[r], r, 0) for r in range(1, near)]
    arrays = regroup(arrays)
    return [arrays[0]] + [shift(arrays[q], 0, q) for q in range(1, far)]


def level_spectra(received, decoded, matrix):
    parts, group, height, lanes = (len(received),) + received[0].shape
    members, cells, levels = decoded.shape
    wide = 2 * lanes
    span = group * wide

    def body(*refs):
        got_refs = refs[:parts]
        dec_ref, mat_ref, o_ref, got_ref, cell_ref, val_ref, acc_ref = refs[parts:]
        for q in range(parts):
            got_ref[q * group : (q + 1) * group] = got_refs[q][...]
        acc_ref[...] = jnp.zeros_like(acc_ref)
        cell_iota = lax.broadcasted_iota(jnp.int32, (cells, wide), 0)
        level_iota = lax.broadcasted_iota(jnp.int32, (levels, wide), 0)

        def one_group(g, carry):
            for u in range(group):
                got = got_ref[g * group + u]
                index = jnp.concatenate(
                    [got[2 * members + 2 : 2 * members + 3], got[2 * members + 3 : 2 * members + 4]], axis=1
                ).astype(jnp.int32)
                cell, level = index // levels, index % levels
                first, second = u * wide, span + u * wide
                hot_cell = (cell_iota == cell).astype(jnp.bfloat16)
                cell_ref[:, first : first + wide] = hot_cell
                cell_ref[:, second : second + wide] = hot_cell
                hot_level = (level_iota == level).astype(jnp.bfloat16)
                weight = jnp.concatenate(
                    [got[2 * members : 2 * members + 1], got[2 * members + 1 : 2 * members + 2]], axis=1
                )
                value = jnp.concatenate([got[:members], got[members : 2 * members]], axis=1)
                full = jnp.concatenate([weight, value], axis=0)
                high = full.astype(jnp.bfloat16)
                low = (full - high.astype(jnp.float32)).astype(jnp.bfloat16)
                for q in range(members + 1):
                    at = slice(q * levels, (q + 1) * levels)
                    val_ref[at, first : first + wide] = hot_level * high[q : q + 1]
                    val_ref[at, second : second + wide] = hot_level * low[q : q + 1]
            acc_ref[...] += dot_nt(cell_ref[...], val_ref[...])
            return carry

        lax.fori_loop(0, parts, one_group, 0)
        weights = acc_ref[:, :levels]
        for q in range(members):
            forcing = weights * dec_ref[q] - acc_ref[:, (q + 1) * levels : (q + 2) * levels]
            o_ref[q] = dot(mat_ref[...], forcing.astype(jnp.bfloat16)).astype(jnp.bfloat16)

    vmem = pl.BlockSpec(memory_space=pltpu.VMEM)
    return pl.pallas_call(
        body,
        out_shape=jax.ShapeDtypeStruct((members, matrix.shape[0], levels), jnp.bfloat16),
        in_specs=[vmem] * (parts + 2),
        out_specs=vmem,
        scratch_shapes=[
            pltpu.VMEM((parts * group, height, lanes), jnp.float32),
            pltpu.VMEM((cells, 2 * span), jnp.bfloat16),
            pltpu.VMEM(((members + 1) * levels, 2 * span), jnp.bfloat16),
            pltpu.VMEM((cells, (members + 1) * levels), jnp.float32),
        ],
        cost_estimate=cost(16 * parts * group * wide * cells * levels, 4 * members * cells * levels),
        name="level_spectra",
    )(*received, decoded, matrix)


def slopes(spectra, merid, mats, bias):
    sections, rows, cols = spectra.shape
    _, chunks, _, width = mats.shape
    half = rows // 2

    def body(x_ref, d_ref, w_ref, b_ref, o_ref):
        for c in range(chunks):
            at = slice(c * width, (c + 1) * width)
            mode = dot(d_ref[...], x_ref[0, :, at]).astype(jnp.bfloat16)
            re, im = mode[:half], mode[half:]
            pre_re = dot(jnp.concatenate([re, -im], axis=1), w_ref[0, c])
            pre_im = dot(jnp.concatenate([im, re], axis=1), w_ref[0, c])
            o_ref[0, :half, at] = gelu_slope(pre_re + b_ref[0:1, at])
            o_ref[0, half:, at] = gelu_slope(pre_im + b_ref[1:2, at])

    part = pl.BlockSpec((1, rows, cols), lambda t: (t, 0, 0))
    return pl.pallas_call(
        body,
        out_shape=jax.ShapeDtypeStruct(spectra.shape, jnp.float32),
        grid=(sections,),
        in_specs=[
            part,
            pl.BlockSpec(merid.shape, lambda t: (0, 0)),
            pl.BlockSpec((1,) + mats.shape[1:], lambda t: (0, 0, 0, 0)),
            pl.BlockSpec(bias.shape, lambda t: (0, 0)),
        ],
        out_specs=part,
        cost_estimate=cost(3 * sections * rows * cols * width, 6 * sections * rows * cols),
        name="slopes",
    )(spectra, merid, mats, bias)


def sweep(slope, level_spec, merid, merid_t, herm, mats, decoder):
    sections, rows, cols = slope.shape
    _, chunks, _, width = mats.shape
    levels = decoder.shape[1]
    half = rows // 2

    def body(x_ref, f_ref, d_ref, dt_ref, h_ref, w_ref, dec_ref, o_ref, seen_ref, all_ref):
        @pl.when(pl.program_id(0) == 0)
        def _():
            seen_ref[...] = jnp.zeros_like(seen_ref)
            all_ref[...] = jnp.zeros_like(all_ref)

        def crossed(array):
            re, im = array[:half], array[half:]
            return jnp.concatenate(
                [jnp.concatenate([re, im], axis=1), jnp.concatenate([im, -re], axis=1)], axis=0
            )

        forced = dot(d_ref[...], f_ref[0]).astype(jnp.bfloat16)
        forced_seen = dot(h_ref[...], forced).astype(jnp.bfloat16)
        for c in range(chunks):
            at = slice(c * width, (c + 1) * width)
            seen = seen_ref[:, at]
            hid = dot(crossed(seen.astype(jnp.bfloat16)), w_ref[0, c])
            act = (hid * x_ref[0, :, at]).astype(jnp.bfloat16)
            grad = dot(crossed(act), w_ref[1, c]).astype(jnp.bfloat16)
            grad = dot(h_ref[...], grad)
            seen_ref[:, at] = seen + grad + dot_nt(forced_seen, dec_ref[at])
            total = all_ref[:, at] + grad + dot_nt(forced, dec_ref[at])
            all_ref[:, at] = total
            o_ref[0, :, at] = dot(dt_ref[...], total.astype(jnp.bfloat16)).astype(jnp.bfloat16)

    def turn(width):
        return pl.BlockSpec((1, rows, width), lambda t: (sections - 1 - t, 0, 0))

    square = pl.BlockSpec((rows, rows), lambda t: (0, 0))
    return pl.pallas_call(
        body,
        out_shape=jax.ShapeDtypeStruct((sections, rows, cols), jnp.bfloat16),
        grid=(sections,),
        in_specs=[
            turn(cols),
            turn(levels),
            square,
            square,
            square,
            pl.BlockSpec((2,) + mats.shape[1:], lambda t: (0, 0, 0, 0)),
            pl.BlockSpec((cols, levels), lambda t: (0, 0)),
        ],
        out_specs=turn(cols),
        scratch_shapes=[pltpu.VMEM((rows, cols), jnp.float32)] * 2,
        cost_estimate=cost(6 * sections * rows * cols * width, 6 * sections * rows * cols),
        name="sweep",
    )(slope, level_spec, merid, merid_t, herm, mats, decoder)


def swap(array, axis):
    batch, rows, cols = array.shape
    return lax.all_to_all(
        array.reshape(-1, 8, cols), axis, split_axis=0, concat_axis=0, tiled=True
    ).reshape(batch, rows, cols)


def shards(
    states,
    filter_in,
    filter_out,
    filter_bias,
    decoder,
    obs_value,
    obs_weight,
    obs_index,
    block_dest,
    block_count,
):
    member_count, lat_local, lon_len, channels = states.shape[1:]
    tiles = lax.axis_size("space")
    tables = {
        name: jnp.asarray(table, jnp.bfloat16)
        for name, table in make_matrices(tiles, lat_local, lon_len).items()
    }
    fields = states.reshape(member_count, lat_local * lon_len, channels)
    near = math.gcd(tiles, 4)
    far = tiles // near
    here = lax.axis_index("space").astype(jnp.int32)
    spectra = swap(mix_rows(tables["state"], fields), EVERY)
    outbox = pack_outbox(
        obs_value[0], obs_weight, obs_index, block_dest[0], block_count[0], here[None], near, far
    )
    received = route(outbox, near, far)
    decoded = jnp.einsum("mnc,cv->mnv", fields, decoder, preferred_element_type=jnp.float32)
    levels = level_spectra(received, decoded, tables["force"])
    spectra, levels = lax.optimization_barrier((spectra, levels))
    levels = swap(levels, EVERY)
    forward, adjoint = dense_blocks(filter_in, filter_out, 2)
    herm = jnp.where(here == 0, tables["herm"], jnp.eye(tables["herm"].shape[0], dtype=jnp.bfloat16))
    slope = slopes(spectra, tables["merid"], forward, filter_bias)
    swept = sweep(slope, levels, tables["merid"], tables["merid_t"], herm, adjoint, decoder)
    result = mix_rows(tables["back"], swap(swept, EVERY))
    return result.reshape(1, member_count, lat_local, lon_len, channels)


def solution(mesh):
    placed = (
        P("lead", None, "space", None, None),
        P(),
        P(),
        P(),
        P(),
        P("lead", None, "space"),
        P("lead", "space"),
        P("lead", "space"),
        P("lead", "space"),
        P("lead", "space"),
    )
    return jax.shard_map(
        shards,
        mesh=mesh,
        in_specs=placed,
        out_specs=P("lead", None, "space", None, None),
        check_vma=False,
    )
```

```python
import math

import jax
import jax.numpy as jnp
import numpy as np
from jax import lax
from jax.experimental import pallas as pl
from jax.experimental.pallas import tpu as pltpu
from jax.sharding import PartitionSpec as P

OBS_BLK = 128
EVERY = ("lead", "space")

root_scale = math.sqrt(2.0 / math.pi)
cubic_term = 0.044715


def gelu_slope(values):
    square = values * values
    tangent = jnp.tanh(values * (root_scale + (root_scale * cubic_term) * square))
    bend = values * ((0.5 * root_scale) + (1.5 * root_scale * cubic_term) * square)
    return 0.5 + 0.5 * tangent + bend * (1.0 - tangent * tangent)


def waves(rows, cols, length):
    angle = (np.outer(np.arange(rows), np.arange(cols)) % length) * (2.0 * math.pi / length)
    return np.cos(angle), np.sin(angle)


def make_matrices(tiles, lat_local, lon_len):
    lat_len, modes = tiles * lat_local, lon_len // 2
    pair = modes // tiles
    cos, sin = waves(modes, lon_len, lon_len)
    scale = 1.0 / math.sqrt(lon_len)
    gain = np.where(np.arange(modes) == 0, 1.0, 2.0)[:, None]
    nyquist = np.cos(math.pi * np.arange(lon_len)) * scale

    def zonal(factor, full):
        parts = np.stack([factor * cos * scale, -factor * sin * scale])
        parts[1, 0] = nyquist if full else 0.0
        parts = parts.reshape(2, tiles, pair, lon_len).transpose(1, 0, 2, 3)
        out = np.zeros((tiles, lat_local, 2, pair, lat_local, lon_len))
        for f in range(lat_local):
            out[:, f, :, :, f] = parts
        return out.reshape(tiles * lat_local * 2 * pair, lat_local * lon_len)

    lat_cos, lat_sin = (t / math.sqrt(lat_len) for t in waves(lat_len, lat_len, lat_len))
    merid = np.zeros((2, pair, lat_len, lat_len, 2, pair))
    for k in range(pair):
        merid[0, k, :, :, 0, k] = lat_cos
        merid[0, k, :, :, 1, k] = lat_sin
        merid[1, k, :, :, 0, k] = -lat_sin
        merid[1, k, :, :, 1, k] = lat_cos
    middle = lat_len // 2
    order = np.concatenate([np.arange(middle), [middle], np.arange(lat_len - 1, middle, -1)])
    merid = merid[:, :, order].reshape(2 * pair * lat_len, lat_len * 2 * pair)
    keep = np.ones((2, pair, lat_len, 1))
    take = np.zeros((2, pair, lat_len, 1))
    paired = (order % middle != 0)[:, None]
    keep[0, 0] = np.where(paired, 0.5, 1.0)
    take[0, 0] = np.where(paired, 0.5, 0.0)
    keep[1, 0] = np.where(paired, 0.5, 0.0)
    take[1, 0] = np.where(paired, -0.5, 0.0)
    herm = np.stack([keep, take]).reshape(2, 2 * pair * lat_len, 1)
    return {
        "state": zonal(1.0, False).astype(np.float32),
        "force": zonal(gain, True).astype(np.float32),
        "back": zonal(1.0, True).T.astype(np.float32),
        "merid": merid.astype(np.float32),
        "merid_t": merid.T.astype(np.float32),
        "herm": np.broadcast_to(herm, herm.shape[:2] + (128,)).astype(np.float32),
    }


def dot(a, b):
    return lax.dot_general(a, b, (((1,), (0,)), ((), ())), preferred_element_type=jnp.float32)


def dot_nt(a, b):
    return lax.dot_general(a, b, (((1,), (1,)), ((), ())), preferred_element_type=jnp.float32)


def cost(products, moved):
    return pl.CostEstimate(flops=2 * products, transcendentals=0, bytes_accessed=moved)


def mix_rows(matrix, array, per_step=4):
    batch, rows, cols = array.shape

    def body(m_ref, x_ref, o_ref):
        for u in range(per_step):
            o_ref[u] = dot(m_ref[...], x_ref[u]).astype(jnp.bfloat16)

    part = pl.BlockSpec((per_step, rows, cols), lambda b: (b, 0, 0))
    return pl.pallas_call(
        body,
        out_shape=jax.ShapeDtypeStruct(array.shape, jnp.bfloat16),
        grid=(batch // per_step,),
        in_specs=[pl.BlockSpec((rows, rows), lambda b: (0, 0)), part],
        out_specs=part,
        cost_estimate=cost(batch * rows * rows * cols, 4 * batch * rows * cols),
        name="mix_rows",
    )(matrix, array)


def dense_blocks(filter_in, filter_out, chunks):
    _, blocks, size, _ = filter_in.shape
    per = blocks // chunks
    width = per * size
    lift = np.tile(np.eye(size, dtype=np.float32), (per, 1))
    same = np.kron(np.eye(per, dtype=np.float32), np.ones((size, size), np.float32))

    def body(in_ref, out_ref, lift_ref, same_ref, f_ref, a_ref):
        same_block = same_ref[...]
        for c in range(chunks):
            for q in range(2):
                at = slice(q * width, (q + 1) * width)
                w_in = in_ref[q, c * per : (c + 1) * per].reshape(width, size)
                w_out = out_ref[q, c * per : (c + 1) * per].reshape(width, size)
                f_ref[0, c, at] = (dot_nt(w_in, lift_ref[...]) * same_block).astype(jnp.bfloat16)
                a_ref[0, c, at] = (dot_nt(lift_ref[...], w_out) * same_block).astype(jnp.bfloat16)
                a_ref[1, c, at] = (dot_nt(lift_ref[...], w_in) * same_block).astype(jnp.bfloat16)

    vmem = pl.BlockSpec(memory_space=pltpu.VMEM)
    return pl.pallas_call(
        body,
        out_shape=(
            jax.ShapeDtypeStruct((1, chunks, 2 * width, width), jnp.bfloat16),
            jax.ShapeDtypeStruct((2, chunks, 2 * width, width), jnp.bfloat16),
        ),
        in_specs=[vmem] * 4,
        out_specs=(vmem, vmem),
        cost_estimate=cost(12 * width * width * size, 12 * width * width),
        name="dense_blocks",
    )(filter_in, filter_out, jnp.asarray(lift, jnp.bfloat16), jnp.asarray(same, jnp.float32))


def pack_outbox(obs_value, obs_weight, obs_index, block_dest, block_count, tiles):
    members, rows = obs_value.shape
    blocks = rows // OBS_BLK

    def body(dest_ref, count_ref, value_ref, weight_ref, index_ref, o_ref, seen_ref):
        o_ref[...] = jnp.zeros_like(o_ref)
        lane = lax.broadcasted_iota(jnp.int32, (1, OBS_BLK), 1)
        for t in range(tiles):
            seen_ref[t] = 0
        for b in range(blocks):
            tile = dest_ref[b]
            rank = seen_ref[tile]
            seen_ref[tile] = rank + 1
            span = slice(b * OBS_BLK, (b + 1) * OBS_BLK)
            weight = jnp.where(lane < count_ref[b], weight_ref[:, span], 0.0)
            o_ref[tile, pl.ds(pl.multiple_of(rank * members, members), members), :] = (
                value_ref[:, span] * weight
            )
            o_ref[tile, pl.ds(2 * members + rank, 1), :] = weight
            o_ref[tile, pl.ds(2 * members + 2 + rank, 1), :] = index_ref[:, span].astype(jnp.float32)

    smem = pl.BlockSpec(memory_space=pltpu.SMEM)
    vmem = pl.BlockSpec(memory_space=pltpu.VMEM)
    return pl.pallas_call(
        body,
        out_shape=jax.ShapeDtypeStruct((tiles, 2 * members + 8, OBS_BLK), jnp.float32),
        in_specs=[smem, smem, vmem, vmem, vmem],
        out_specs=vmem,
        scratch_shapes=[pltpu.SMEM((tiles,), jnp.int32)],
        name="pack_outbox",
    )(block_dest, block_count, obs_value, obs_weight, obs_index)


def level_spectra(received, decoded, matrix):
    sources, _, lanes = received.shape
    group = 4
    members, cells, levels = decoded.shape
    wide = 2 * lanes
    span = group * wide

    def body(got_ref, dec_ref, mat_ref, o_ref, cell_ref, val_ref, acc_ref):
        acc_ref[...] = jnp.zeros_like(acc_ref)
        cell_iota = lax.broadcasted_iota(jnp.int32, (cells, wide), 0)
        level_iota = lax.broadcasted_iota(jnp.int32, (levels, wide), 0)

        def one_group(g, carry):
            for u in range(group):
                got = got_ref[g * group + u]
                index = jnp.concatenate(
                    [got[2 * members + 2 : 2 * members + 3], got[2 * members + 3 : 2 * members + 4]], axis=1
                ).astype(jnp.int32)
                cell, level = index // levels, index % levels
                first, second = u * wide, span + u * wide
                hot_cell = (cell_iota == cell).astype(jnp.bfloat16)
                cell_ref[:, first : first + wide] = hot_cell
                cell_ref[:, second : second + wide] = hot_cell
                hot_level = (level_iota == level).astype(jnp.bfloat16)
                weight = jnp.concatenate(
                    [got[2 * members : 2 * members + 1], got[2 * members + 1 : 2 * members + 2]], axis=1
                )
                value = jnp.concatenate([got[:members], got[members : 2 * members]], axis=1)
                full = jnp.concatenate([weight, value], axis=0)
                high = full.astype(jnp.bfloat16)
                low = (full - high.astype(jnp.float32)).astype(jnp.bfloat16)
                for q in range(members + 1):
                    at = slice(q * levels, (q + 1) * levels)
                    val_ref[at, first : first + wide] = hot_level * high[q : q + 1]
                    val_ref[at, second : second + wide] = hot_level * low[q : q + 1]
            acc_ref[...] += dot_nt(cell_ref[...], val_ref[...])
            return carry

        lax.fori_loop(0, sources // group, one_group, 0)
        weights = acc_ref[:, :levels]
        for q in range(members):
            forcing = weights * dec_ref[q] - acc_ref[:, (q + 1) * levels : (q + 2) * levels]
            o_ref[q] = dot(mat_ref[...], forcing.astype(jnp.bfloat16)).astype(jnp.bfloat16)

    vmem = pl.BlockSpec(memory_space=pltpu.VMEM)
    return pl.pallas_call(
        body,
        out_shape=jax.ShapeDtypeStruct((members, matrix.shape[0], levels), jnp.bfloat16),
        in_specs=[vmem] * 3,
        out_specs=vmem,
        scratch_shapes=[
            pltpu.VMEM((cells, 2 * span), jnp.bfloat16),
            pltpu.VMEM(((members + 1) * levels, 2 * span), jnp.bfloat16),
            pltpu.VMEM((cells, (members + 1) * levels), jnp.float32),
        ],
        cost_estimate=cost(16 * sources * wide * cells * levels, 4 * members * cells * levels),
        name="level_spectra",
    )(received, decoded, matrix)


def slopes(spectra, merid, mats, bias):
    sections, rows, cols = spectra.shape
    _, chunks, _, width = mats.shape
    half = rows // 2

    def body(x_ref, d_ref, w_ref, b_ref, o_ref):
        for c in range(chunks):
            at = slice(c * width, (c + 1) * width)
            mode = dot(d_ref[...], x_ref[0, :, at]).astype(jnp.bfloat16)
            re, im = mode[:half], mode[half:]
            pre_re = dot(jnp.concatenate([re, -im], axis=1), w_ref[0, c])
            pre_im = dot(jnp.concatenate([im, re], axis=1), w_ref[0, c])
            o_ref[0, :half, at] = gelu_slope(pre_re + b_ref[0:1, at])
            o_ref[0, half:, at] = gelu_slope(pre_im + b_ref[1:2, at])

    part = pl.BlockSpec((1, rows, cols), lambda t: (t, 0, 0))
    return pl.pallas_call(
        body,
        out_shape=jax.ShapeDtypeStruct(spectra.shape, jnp.float32),
        grid=(sections,),
        in_specs=[
            part,
            pl.BlockSpec(merid.shape, lambda t: (0, 0)),
            pl.BlockSpec((1,) + mats.shape[1:], lambda t: (0, 0, 0, 0)),
            pl.BlockSpec(bias.shape, lambda t: (0, 0)),
        ],
        out_specs=part,
        cost_estimate=cost(3 * sections * rows * cols * width, 6 * sections * rows * cols),
        name="slopes",
    )(spectra, merid, mats, bias)


def sweep(slope, level_spec, merid, merid_t, herm, mats, decoder, group):
    sections, rows, cols = slope.shape
    _, chunks, _, width = mats.shape
    levels = decoder.shape[1]
    half = rows // 2

    def body(x_ref, f_ref, d_ref, dt_ref, h_ref, w_ref, dec_ref, o_ref, z_ref):
        @pl.when(pl.program_id(0) == 0)
        def _():
            z_ref[...] = jnp.zeros_like(z_ref)

        keep = jnp.concatenate([h_ref[0]] * (width // h_ref.shape[2]), axis=1)
        take = jnp.concatenate([h_ref[1]] * (width // h_ref.shape[2]), axis=1)

        def hermitian(array):
            parts = []
            for g in range(0, rows, group):
                parts += [array[g + group // 2 : g + group], array[g : g + group // 2]]
            return keep * array + take * jnp.concatenate(parts, axis=0)

        def crossed(array):
            array = array.astype(jnp.bfloat16)
            re, im = array[:half], array[half:]
            return jnp.concatenate(
                [jnp.concatenate([re, im], axis=1), jnp.concatenate([im, -re], axis=1)], axis=0
            )

        spans = [slice(c * width, (c + 1) * width) for c in range(chunks)]
        forced = dot(d_ref[...], f_ref[0]).astype(jnp.bfloat16)
        hids = [
            dot(crossed(hermitian(z_ref[:, at])), w_ref[0, c]) for c, at in enumerate(spans)
        ]
        pushed = [z_ref[:, at] + dot_nt(forced, dec_ref[at]) for at in spans]
        grads = [
            dot(crossed(hids[c] * x_ref[0, :, at]), w_ref[1, c]) for c, at in enumerate(spans)
        ]
        for c, at in enumerate(spans):
            total = pushed[c] + hermitian(grads[c])
            z_ref[:, at] = total
            o_ref[0, :, at] = dot(dt_ref[...], total.astype(jnp.bfloat16)).astype(jnp.bfloat16)

    def turn(width):
        return pl.BlockSpec((1, rows, width), lambda t: (sections - 1 - t, 0, 0))

    square = pl.BlockSpec((rows, rows), lambda t: (0, 0))
    return pl.pallas_call(
        body,
        out_shape=jax.ShapeDtypeStruct((sections, rows, cols), jnp.bfloat16),
        grid=(sections,),
        in_specs=[
            turn(cols),
            turn(levels),
            square,
            square,
            pl.BlockSpec(herm.shape, lambda t: (0, 0, 0)),
            pl.BlockSpec((2,) + mats.shape[1:], lambda t: (0, 0, 0, 0)),
            pl.BlockSpec((cols, levels), lambda t: (0, 0)),
        ],
        out_specs=turn(cols),
        scratch_shapes=[pltpu.VMEM((rows, cols), jnp.float32)],
        cost_estimate=cost(6 * sections * rows * cols * width, 6 * sections * rows * cols),
        name="sweep",
    )(slope, level_spec, merid, merid_t, herm, mats, decoder)


def swap(array, axis):
    batch, rows, cols = array.shape
    return lax.all_to_all(
        array.reshape(-1, 8, cols), axis, split_axis=0, concat_axis=0, tiled=True
    ).reshape(batch, rows, cols)


def shards(
    states,
    filter_in,
    filter_out,
    filter_bias,
    decoder,
    obs_value,
    obs_weight,
    obs_index,
    block_dest,
    block_count,
):
    member_count, lat_local, lon_len, channels = states.shape[1:]
    tiles = lax.axis_size("space")
    tables = {
        name: jnp.asarray(table, jnp.float32 if name == "herm" else jnp.bfloat16)
        for name, table in make_matrices(tiles, lat_local, lon_len).items()
    }
    fields = states.reshape(member_count, lat_local * lon_len, channels)
    outbox = pack_outbox(obs_value[0], obs_weight, obs_index, block_dest[0], block_count[0], tiles)
    received = lax.all_to_all(outbox, "space", split_axis=0, concat_axis=0, tiled=True)
    mixed = mix_rows(tables["state"], fields)
    mixed, received = lax.optimization_barrier((mixed, received))
    spectra = swap(mixed, EVERY)
    decoded = jnp.einsum("mnc,cv->mnv", fields, decoder, preferred_element_type=jnp.float32)
    levels = level_spectra(received, decoded, tables["force"])
    spectra, levels = lax.optimization_barrier((spectra, levels))
    levels = swap(levels, EVERY)
    forward, adjoint = dense_blocks(filter_in, filter_out, 2)
    plain = np.zeros(tables["herm"].shape, np.float32)
    plain[0] = 1.0
    herm = jnp.where(lax.axis_index("space") == 0, tables["herm"], plain)
    slope = slopes(spectra, tables["merid"], forward, filter_bias)
    swept = sweep(
        slope,
        levels,
        tables["merid"],
        tables["merid_t"],
        herm,
        adjoint,
        decoder,
        tiles * lat_local,
    )
    result = mix_rows(tables["back"], swap(swept, EVERY))
    return result.reshape(1, member_count, lat_local, lon_len, channels)


def solution(mesh):
    placed = (
        P("lead", None, "space", None, None),
        P(),
        P(),
        P(),
        P(),
        P("lead", None, "space"),
        P("lead", "space"),
        P("lead", "space"),
        P("lead", "space"),
        P("lead", "space"),
    )
    return jax.shard_map(
        shards,
        mesh=mesh,
        in_specs=placed,
        out_specs=P("lead", None, "space", None, None),
        check_vma=False,
    )
```

```python
import math

import jax
import jax.numpy as jnp
import numpy as np
from jax import lax
from jax.experimental import pallas as pl
from jax.experimental.pallas import tpu as pltpu
from jax.sharding import PartitionSpec as P

OBS_BLK = 128
EVERY = ("lead", "space")

root_scale = math.sqrt(2.0 / math.pi)
cubic_term = 0.044715


def gelu_slope(values):
    square = values * values
    tangent = jnp.tanh(values * (root_scale + (root_scale * cubic_term) * square))
    bend = values * ((0.5 * root_scale) + (1.5 * root_scale * cubic_term) * square)
    return 0.5 + 0.5 * tangent + bend * (1.0 - tangent * tangent)


def waves(rows, cols, length):
    angle = (np.outer(np.arange(rows), np.arange(cols)) % length) * (2.0 * math.pi / length)
    return np.cos(angle), np.sin(angle)


def make_matrices(tiles, lat_local, lon_len):
    lat_len, modes = tiles * lat_local, lon_len // 2
    pair = modes // tiles
    cos, sin = waves(modes, lon_len, lon_len)
    scale = 1.0 / math.sqrt(lon_len)
    gain = np.where(np.arange(modes) == 0, 1.0, 2.0)[:, None]
    nyquist = np.cos(math.pi * np.arange(lon_len)) * scale

    def zonal(factor, full):
        parts = np.stack([factor * cos * scale, -factor * sin * scale])
        parts[1, 0] = nyquist if full else 0.0
        parts = parts.reshape(2, tiles, pair, lon_len).transpose(1, 0, 2, 3)
        out = np.zeros((tiles, lat_local, 2, pair, lat_local, lon_len))
        for f in range(lat_local):
            out[:, f, :, :, f] = parts
        return out.reshape(tiles * lat_local * 2 * pair, lat_local * lon_len)

    lat_cos, lat_sin = (t / math.sqrt(lat_len) for t in waves(lat_len, lat_len, lat_len))
    merid = np.zeros((2, pair, lat_len, lat_len, 2, pair))
    for k in range(pair):
        merid[0, k, :, :, 0, k] = lat_cos
        merid[0, k, :, :, 1, k] = lat_sin
        merid[1, k, :, :, 0, k] = -lat_sin
        merid[1, k, :, :, 1, k] = lat_cos
    middle = lat_len // 2
    order = np.concatenate([np.arange(middle), [middle], np.arange(lat_len - 1, middle, -1)])
    merid = merid[:, :, order].reshape(2 * pair * lat_len, lat_len * 2 * pair)
    keep = np.ones((2, pair, lat_len, 1))
    take = np.zeros((2, pair, lat_len, 1))
    paired = (order % middle != 0)[:, None]
    keep[0, 0] = np.where(paired, 0.5, 1.0)
    take[0, 0] = np.where(paired, 0.5, 0.0)
    keep[1, 0] = np.where(paired, 0.5, 0.0)
    take[1, 0] = np.where(paired, -0.5, 0.0)
    herm = np.stack([keep, take]).reshape(2, 2 * pair * lat_len, 1)
    return {
        "state": zonal(1.0, False).astype(np.float32),
        "force": zonal(gain, True).astype(np.float32),
        "back": zonal(1.0, True).T.astype(np.float32),
        "merid": merid.astype(np.float32),
        "merid_t": merid.T.astype(np.float32),
        "herm": herm.astype(np.float32),
    }


def dot(a, b):
    return lax.dot_general(a, b, (((1,), (0,)), ((), ())), preferred_element_type=jnp.float32)


def dot_nt(a, b):
    return lax.dot_general(a, b, (((1,), (1,)), ((), ())), preferred_element_type=jnp.float32)


def cost(products, moved):
    return pl.CostEstimate(flops=2 * products, transcendentals=0, bytes_accessed=moved)


def mix_rows(matrix, array, per_step=4):
    batch, rows, cols = array.shape

    def body(m_ref, x_ref, o_ref):
        for u in range(per_step):
            o_ref[u] = dot(m_ref[...], x_ref[u]).astype(jnp.bfloat16)

    part = pl.BlockSpec((per_step, rows, cols), lambda b: (b, 0, 0))
    return pl.pallas_call(
        body,
        out_shape=jax.ShapeDtypeStruct(array.shape, jnp.bfloat16),
        grid=(batch // per_step,),
        in_specs=[pl.BlockSpec((rows, rows), lambda b: (0, 0)), part],
        out_specs=part,
        cost_estimate=cost(batch * rows * rows * cols, 4 * batch * rows * cols),
        name="mix_rows",
    )(matrix, array)


def dense_blocks(filter_in, filter_out, chunks):
    _, blocks, size, _ = filter_in.shape
    per = blocks // chunks
    width = per * size

    def body(in_ref, out_ref, f_ref, a_ref):
        row = lax.broadcasted_iota(jnp.int32, (width, width), 0)
        col = lax.broadcasted_iota(jnp.int32, (width, width), 1)
        same_block = (row // size == col // size).astype(jnp.float32)
        row = lax.broadcasted_iota(jnp.int32, (width, size), 0)
        col = lax.broadcasted_iota(jnp.int32, (width, size), 1)
        lift = (row % size == col).astype(jnp.bfloat16)
        for c in range(chunks):
            for q in range(2):
                at = slice(q * width, (q + 1) * width)
                w_in = in_ref[q, c * per : (c + 1) * per].reshape(width, size)
                w_out = out_ref[q, c * per : (c + 1) * per].reshape(width, size)
                f_ref[0, c, at] = (dot_nt(w_in, lift) * same_block).astype(jnp.bfloat16)
                a_ref[0, c, at] = (dot_nt(lift, w_out) * same_block).astype(jnp.bfloat16)
                a_ref[1, c, at] = (dot_nt(lift, w_in) * same_block).astype(jnp.bfloat16)

    vmem = pl.BlockSpec(memory_space=pltpu.VMEM)
    return pl.pallas_call(
        body,
        out_shape=(
            jax.ShapeDtypeStruct((1, chunks, 2 * width, width), jnp.bfloat16),
            jax.ShapeDtypeStruct((2, chunks, 2 * width, width), jnp.bfloat16),
        ),
        in_specs=[vmem] * 2,
        out_specs=(vmem, vmem),
        cost_estimate=cost(12 * width * width * size, 12 * width * width),
        name="dense_blocks",
    )(filter_in, filter_out)


def pack_outbox(obs_value, obs_weight, obs_index, block_dest, block_count, tiles):
    members, rows = obs_value.shape
    blocks = rows // OBS_BLK

    def body(dest_ref, count_ref, value_ref, weight_ref, index_ref, o_ref, seen_ref):
        o_ref[...] = jnp.zeros_like(o_ref)
        lane = lax.broadcasted_iota(jnp.int32, (1, OBS_BLK), 1)
        for t in range(tiles):
            seen_ref[t] = 0
        for b in range(blocks):
            tile = dest_ref[b]
            rank = seen_ref[tile]
            seen_ref[tile] = rank + 1
            span = slice(b * OBS_BLK, (b + 1) * OBS_BLK)
            weight = jnp.where(lane < count_ref[b], weight_ref[:, span], 0.0)
            o_ref[tile, pl.ds(pl.multiple_of(rank * members, members), members), :] = (
                value_ref[:, span] * weight
            )
            o_ref[tile, pl.ds(2 * members + rank, 1), :] = weight
            o_ref[tile, pl.ds(2 * members + 2 + rank, 1), :] = index_ref[:, span].astype(jnp.float32)

    smem = pl.BlockSpec(memory_space=pltpu.SMEM)
    vmem = pl.BlockSpec(memory_space=pltpu.VMEM)
    return pl.pallas_call(
        body,
        out_shape=jax.ShapeDtypeStruct((tiles, 2 * members + 8, OBS_BLK), jnp.float32),
        in_specs=[smem, smem, vmem, vmem, vmem],
        out_specs=vmem,
        scratch_shapes=[pltpu.SMEM((tiles,), jnp.int32)],
        name="pack_outbox",
    )(block_dest, block_count, obs_value, obs_weight, obs_index)


def regroup(arrays, pieces, rows):
    count = len(arrays)
    lead, height, lanes = arrays[0].shape
    shape = (count, height, lanes) if rows is None else (count, lead, rows, lanes)

    def body(*refs):
        for q in range(pieces):
            for r in range(count):
                if rows is None:
                    refs[count + q][r] = refs[r][q]
                else:
                    refs[count + q][r] = refs[r][:, q * rows : (q + 1) * rows]

    vmem = pl.BlockSpec(memory_space=pltpu.VMEM)
    return pl.pallas_call(
        body,
        out_shape=[jax.ShapeDtypeStruct(shape, arrays[0].dtype)] * pieces,
        in_specs=[vmem] * count,
        out_specs=[vmem] * pieces,
        name="regroup",
    )(*arrays)


def route(arrays, near, far):
    members = len(arrays)

    def shift(array, by_near, by_far):
        perm = [
            (z * near + y, (z + by_far) % far * near + (y + by_near) % near)
            for z in range(far)
            for y in range(near)
        ]
        return lax.ppermute(array, "space", perm)

    def ahead(array, by):
        return lax.ppermute(array, "lead", [(l, (l + by) % members) for l in range(members)])

    arrays = [arrays[0]] + [ahead(arrays[d], d) for d in range(1, members)]
    arrays = regroup(arrays, near, None)
    arrays = [arrays[0]] + [shift(arrays[r], r, 0) for r in range(1, near)]
    arrays = regroup(arrays, far, arrays[0].shape[1] // far)
    moved = [arrays[0]]
    for q in range(1, far):
        with jax.named_scope("far_%d" % q):
            moved.append(shift(arrays[q], 0, q))
    return moved


def level_spectra(received, decoded, matrix, here, near):
    sources, _, lanes = received.shape
    group = 4
    members, cells, levels = decoded.shape
    wide = 2 * lanes
    span = group * wide

    def body(here_ref, got_ref, dec_ref, mat_ref, *rest):
        o_refs, (cell_ref, val_ref, acc_ref) = rest[:members], rest[members:]
        acc_ref[...] = jnp.zeros_like(acc_ref)
        cell_iota = lax.broadcasted_iota(jnp.int32, (cells, wide), 0)
        level_iota = lax.broadcasted_iota(jnp.int32, (levels, wide), 0)

        def one_group(g, carry):
            for u in range(group):
                got = got_ref[g * group + u]
                index = jnp.concatenate(
                    [got[2 * members + 2 : 2 * members + 3], got[2 * members + 3 : 2 * members + 4]], axis=1
                ).astype(jnp.int32)
                cell, level = index // levels, index % levels
                first, second = u * wide, span + u * wide
                hot_cell = (cell_iota == cell).astype(jnp.bfloat16)
                cell_ref[:, first : first + wide] = hot_cell
                cell_ref[:, second : second + wide] = hot_cell
                hot_level = (level_iota == level).astype(jnp.bfloat16)
                weight = jnp.concatenate(
                    [got[2 * members : 2 * members + 1], got[2 * members + 1 : 2 * members + 2]], axis=1
                )
                value = jnp.concatenate([got[:members], got[members : 2 * members]], axis=1)
                full = jnp.concatenate([weight, value], axis=0)
                high = full.astype(jnp.bfloat16)
                low = (full - high.astype(jnp.float32)).astype(jnp.bfloat16)
                for q in range(members + 1):
                    at = slice(q * levels, (q + 1) * levels)
                    val_ref[at, first : first + wide] = hot_level * high[q : q + 1]
                    val_ref[at, second : second + wide] = hot_level * low[q : q + 1]
            acc_ref[...] += dot_nt(cell_ref[...], val_ref[...])
            return carry

        lax.fori_loop(0, sources // group, one_group, 0)
        weights = acc_ref[:, :levels]
        for ahead in range(members):
            member = (here_ref[0] + ahead) % members
            at = pl.multiple_of((member + 1) * levels, levels)
            forcing = weights * dec_ref[member] - acc_ref[:, pl.ds(at, levels)]
            spectrum = dot(mat_ref[...], forcing.astype(jnp.bfloat16)).astype(jnp.bfloat16)
            for r in range(near):
                o_refs[ahead][r] = spectrum[r * part : (r + 1) * part]

    part = matrix.shape[0] // near
    vmem = pl.BlockSpec(memory_space=pltpu.VMEM)
    return pl.pallas_call(
        body,
        out_shape=[jax.ShapeDtypeStruct((near, part, levels), jnp.bfloat16)] * members,
        in_specs=[pl.BlockSpec(memory_space=pltpu.SMEM)] + [vmem] * 3,
        out_specs=[vmem] * members,
        scratch_shapes=[
            pltpu.VMEM((cells, 2 * span), jnp.bfloat16),
            pltpu.VMEM(((members + 1) * levels, 2 * span), jnp.bfloat16),
            pltpu.VMEM((cells, (members + 1) * levels), jnp.float32),
        ],
        cost_estimate=cost(16 * sources * wide * cells * levels, 4 * members * cells * levels),
        name="level_spectra",
    )(here, received, decoded, matrix)


def slopes(spectra, merid, mats, bias):
    sections, rows, cols = spectra.shape
    _, chunks, _, width = mats.shape
    half = rows // 2

    def body(x_ref, d_ref, w_ref, b_ref, o_ref):
        for c in range(chunks):
            at = slice(c * width, (c + 1) * width)
            mode = dot(d_ref[...], x_ref[0, :, at]).astype(jnp.bfloat16)
            re, im = mode[:half], mode[half:]
            pre_re = dot(jnp.concatenate([re, -im], axis=1), w_ref[0, c])
            pre_im = dot(jnp.concatenate([im, re], axis=1), w_ref[0, c])
            o_ref[0, :half, at] = gelu_slope(pre_re + b_ref[0:1, at])
            o_ref[0, half:, at] = gelu_slope(pre_im + b_ref[1:2, at])

    part = pl.BlockSpec((1, rows, cols), lambda t: (t, 0, 0))
    return pl.pallas_call(
        body,
        out_shape=jax.ShapeDtypeStruct(spectra.shape, jnp.float32),
        grid=(sections,),
        in_specs=[
            part,
            pl.BlockSpec(merid.shape, lambda t: (0, 0)),
            pl.BlockSpec((1,) + mats.shape[1:], lambda t: (0, 0, 0, 0)),
            pl.BlockSpec(bias.shape, lambda t: (0, 0)),
        ],
        out_specs=part,
        cost_estimate=cost(3 * sections * rows * cols * width, 6 * sections * rows * cols),
        name="slopes",
    )(spectra, merid, mats, bias)


def sweep(slope, level_spec, merid, merid_t, herm, mats, decoder, here, group):
    sections, rows, cols = slope.shape
    _, chunks, _, width = mats.shape
    levels = decoder.shape[1]
    half = rows // 2

    far, (near, _, height, _) = len(level_spec), level_spec[0].shape

    def body(here_ref, x_ref, d_ref, dt_ref, h_ref, w_ref, dec_ref, *rest):
        f_refs, (o_ref, z_ref, f_ref) = rest[:far], rest[far:]

        @pl.when(pl.program_id(0) == 0)
        def _():
            z_ref[...] = jnp.zeros_like(z_ref)
            for q in range(far):
                for r in range(near):
                    at = (q * near + r) * height
                    f_ref[:, at : at + height] = f_refs[q][r]

        section = sections - 1 - pl.program_id(0)
        back = (here_ref[0] + sections - section) % sections

        keep = jnp.concatenate([h_ref[0]] * (width // h_ref.shape[2]), axis=1)
        take = jnp.concatenate([h_ref[1]] * (width // h_ref.shape[2]), axis=1)

        def hermitian(array):
            parts = []
            for g in range(0, rows, group):
                parts += [array[g + group // 2 : g + group], array[g : g + group // 2]]
            return keep * array + take * jnp.concatenate(parts, axis=0)

        def crossed(array):
            array = array.astype(jnp.bfloat16)
            re, im = array[:half], array[half:]
            return jnp.concatenate(
                [jnp.concatenate([re, im], axis=1), jnp.concatenate([im, -re], axis=1)], axis=0
            )

        spans = [slice(c * width, (c + 1) * width) for c in range(chunks)]
        forced = dot(d_ref[...], f_ref[back]).astype(jnp.bfloat16)
        hids = [
            dot(crossed(hermitian(z_ref[:, at])), w_ref[0, c]) for c, at in enumerate(spans)
        ]
        pushed = [z_ref[:, at] + dot_nt(forced, dec_ref[at]) for at in spans]
        grads = [
            dot(crossed(hids[c] * x_ref[0, :, at]), w_ref[1, c]) for c, at in enumerate(spans)
        ]
        for c, at in enumerate(spans):
            total = pushed[c] + hermitian(grads[c])
            z_ref[:, at] = total
            o_ref[0, :, at] = dot(dt_ref[...], total.astype(jnp.bfloat16)).astype(jnp.bfloat16)

    def turn(width):
        return pl.BlockSpec((1, rows, width), lambda t: (sections - 1 - t, 0, 0))

    square = pl.BlockSpec((rows, rows), lambda t: (0, 0))
    return pl.pallas_call(
        body,
        out_shape=jax.ShapeDtypeStruct((sections, rows, cols), jnp.bfloat16),
        grid=(sections,),
        in_specs=[
            pl.BlockSpec(memory_space=pltpu.SMEM),
            turn(cols),
            square,
            square,
            pl.BlockSpec(herm.shape, lambda t: (0, 0, 0)),
            pl.BlockSpec((2,) + mats.shape[1:], lambda t: (0, 0, 0, 0)),
            pl.BlockSpec((cols, levels), lambda t: (0, 0)),
        ]
        + [pl.BlockSpec(level_spec[0].shape, lambda t: (0, 0, 0, 0))] * far,
        out_specs=turn(cols),
        scratch_shapes=[
            pltpu.VMEM((rows, cols), jnp.float32),
            pltpu.VMEM((sections, rows, levels), jnp.bfloat16),
        ],
        cost_estimate=cost(6 * sections * rows * cols * width, 6 * sections * rows * cols),
        name="sweep",
    )(here, slope, merid, merid_t, herm, mats, decoder, *level_spec)


def swap(array, axis):
    batch, rows, cols = array.shape
    return lax.all_to_all(
        array.reshape(-1, 8, cols), axis, split_axis=0, concat_axis=0, tiled=True
    ).reshape(batch, rows, cols)


def shards(
    states,
    filter_in,
    filter_out,
    filter_bias,
    decoder,
    obs_value,
    obs_weight,
    obs_index,
    block_dest,
    block_count,
):
    member_count, lat_local, lon_len, channels = states.shape[1:]
    tiles = lax.axis_size("space")
    tables = {
        name: jnp.asarray(table, jnp.float32 if name == "herm" else jnp.bfloat16)
        for name, table in make_matrices(tiles, lat_local, lon_len).items()
    }
    fields = states.reshape(member_count, lat_local * lon_len, channels)
    near = math.gcd(tiles, 4)
    far = tiles // near
    lead = lax.axis_index("lead").astype(jnp.int32)[None]
    tile = lax.axis_index("space").astype(jnp.int32)
    row = jnp.arange(tables["force"].shape[0], dtype=jnp.int32)
    high = row.shape[0] // tiles
    step_near, step_far = row // (far * high), row // high % far
    source = (tile // near + step_far) % far * near + (tile % near + step_near) % near
    picked = (source * high + row % high)[:, None] == row[None, :]
    force = dot(picked.astype(jnp.bfloat16), tables["force"]).astype(jnp.bfloat16)
    step_far, step_near = row // (near * high), row // high % near
    source = (tile // near + far - step_far) % far * near + (tile % near + near - step_near) % near
    picked = row[:, None] == (source * high + row % high)[None, :]
    merid = dot(tables["merid"], picked.astype(jnp.bfloat16)).astype(jnp.bfloat16)

    outbox = pack_outbox(obs_value[0], obs_weight, obs_index, block_dest[0], block_count[0], tiles)
    received = lax.all_to_all(outbox, "space", split_axis=0, concat_axis=0, tiled=True)
    mixed = mix_rows(tables["state"], fields)
    mixed, received = lax.optimization_barrier((mixed, received))
    spectra = swap(mixed, EVERY)
    decoded = jnp.einsum("mnc,cv->mnv", fields, decoder, preferred_element_type=jnp.float32)
    levels = route(level_spectra(received, decoded, force, lead, near), near, far)
    forward, adjoint = dense_blocks(filter_in, filter_out, 2)
    plain = np.zeros(tables["herm"].shape, np.float32)
    plain[0] = 1.0
    herm = jnp.broadcast_to(jnp.where(tile == 0, tables["herm"], plain), plain.shape[:2] + (128,))
    slope = slopes(spectra, tables["merid"], forward, filter_bias)
    swept = sweep(
        slope, levels, merid, tables["merid_t"], herm, adjoint, decoder, lead, tiles * lat_local
    )
    result = mix_rows(tables["back"], swap(swept, EVERY))
    return result.reshape(1, member_count, lat_local, lon_len, channels)


def solution(mesh):
    placed = (
        P("lead", None, "space", None, None),
        P(),
        P(),
        P(),
        P(),
        P("lead", None, "space"),
        P("lead", "space"),
        P("lead", "space"),
        P("lead", "space"),
        P("lead", "space"),
    )
    return jax.shard_map(
        shards,
        mesh=mesh,
        in_specs=placed,
        out_specs=P("lead", None, "space", None, None),
        check_vma=False,
    )
```

```python
import math

import jax
import jax.numpy as jnp
import numpy as np
from jax import lax
from jax.experimental import pallas as pl
from jax.experimental.pallas import tpu as pltpu
from jax.sharding import PartitionSpec as P

OBS_BLK = 128
EVERY = ("lead", "space")

root_scale = math.sqrt(2.0 / math.pi)
cubic_term = 0.044715


def gelu_slope(values):
    square = values * values
    tangent = jnp.tanh(values * (root_scale + (root_scale * cubic_term) * square))
    bend = values * ((0.5 * root_scale) + (1.5 * root_scale * cubic_term) * square)
    return 0.5 + 0.5 * tangent + bend * (1.0 - tangent * tangent)


def waves(rows, cols, length):
    angle = (np.outer(np.arange(rows), np.arange(cols)) % length) * (2.0 * math.pi / length)
    return np.cos(angle), np.sin(angle)


def make_matrices(tiles, lat_local, lon_len):
    lat_len, modes = tiles * lat_local, lon_len // 2
    pair = modes // tiles
    cos, sin = waves(modes, lon_len, lon_len)
    scale = 1.0 / math.sqrt(lon_len)
    gain = np.where(np.arange(modes) == 0, 1.0, 2.0)[:, None]
    nyquist = np.cos(math.pi * np.arange(lon_len)) * scale

    def zonal(factor, full):
        parts = np.stack([factor * cos * scale, -factor * sin * scale])
        parts[1, 0] = nyquist if full else 0.0
        parts = parts.reshape(2, tiles, pair, lon_len).transpose(1, 0, 2, 3)
        out = np.zeros((tiles, lat_local, 2, pair, lat_local, lon_len))
        for f in range(lat_local):
            out[:, f, :, :, f] = parts
        return out.reshape(tiles * lat_local * 2 * pair, lat_local * lon_len)

    lat_cos, lat_sin = (t / math.sqrt(lat_len) for t in waves(lat_len, lat_len, lat_len))
    merid = np.zeros((2, pair, lat_len, lat_len, 2, pair))
    for k in range(pair):
        merid[0, k, :, :, 0, k] = lat_cos
        merid[0, k, :, :, 1, k] = lat_sin
        merid[1, k, :, :, 0, k] = -lat_sin
        merid[1, k, :, :, 1, k] = lat_cos
    middle = lat_len // 2
    order = np.concatenate([np.arange(middle), [middle], np.arange(lat_len - 1, middle, -1)])
    merid = merid[:, :, order].reshape(2 * pair * lat_len, lat_len * 2 * pair)
    return {
        "state": zonal(1.0, False).astype(np.float32),
        "force": zonal(gain, True).astype(np.float32),
        "back": zonal(1.0, True).T.astype(np.float32),
        "merid": merid.astype(np.float32),
        "merid_t": merid.T.astype(np.float32),
    }


def dot(a, b):
    return lax.dot_general(a, b, (((1,), (0,)), ((), ())), preferred_element_type=jnp.float32)


def dot_nt(a, b):
    return lax.dot_general(a, b, (((1,), (1,)), ((), ())), preferred_element_type=jnp.float32)


def cost(products, moved):
    return pl.CostEstimate(flops=2 * products, transcendentals=0, bytes_accessed=moved)


def mix_rows(matrix, array, per_step=4):
    batch, rows, cols = array.shape

    def body(m_ref, x_ref, o_ref):
        for u in range(per_step):
            o_ref[u] = dot(m_ref[...], x_ref[u]).astype(jnp.bfloat16)

    part = pl.BlockSpec((per_step, rows, cols), lambda b: (b, 0, 0))
    return pl.pallas_call(
        body,
        out_shape=jax.ShapeDtypeStruct(array.shape, jnp.bfloat16),
        grid=(batch // per_step,),
        in_specs=[pl.BlockSpec((rows, rows), lambda b: (0, 0)), part],
        out_specs=part,
        cost_estimate=cost(batch * rows * rows * cols, 4 * batch * rows * cols),
        name="mix_rows",
    )(matrix, array)


def dense_blocks(filter_in, filter_out, chunks):
    _, blocks, size, _ = filter_in.shape
    per = blocks // chunks
    width = per * size
    window, offset = 2 * width // 3, width // 3

    def body(in_ref, out_ref, f_ref, a_ref):
        row = lax.broadcasted_iota(jnp.int32, (width, width), 0)
        col = lax.broadcasted_iota(jnp.int32, (width, width), 1)
        same = row // size == col // size
        masks = [
            (same & (row < width // 2)).astype(jnp.float32),
            (same & (row >= width // 2)).astype(jnp.float32),
        ]
        row = lax.broadcasted_iota(jnp.int32, (width, size), 0)
        col = lax.broadcasted_iota(jnp.int32, (width, size), 1)
        lift = (row % size == col).astype(jnp.bfloat16)
        for c in range(chunks):
            for q in range(2):
                w_in = in_ref[q, c * per : (c + 1) * per].reshape(width, size)
                w_out = out_ref[q, c * per : (c + 1) * per].reshape(width, size)
                spread = [dot_nt(w_in, lift), dot_nt(lift, w_out), dot_nt(lift, w_in)]
                targets = [f_ref.at[0], a_ref.at[0], a_ref.at[1]]
                for whole, target in zip(spread, targets):
                    for g in range(2):
                        at = slice(g * offset, g * offset + window)
                        target[c, g, q * window : (q + 1) * window] = (
                            (whole * masks[g])[at, at].astype(jnp.bfloat16)
                        )

    vmem = pl.BlockSpec(memory_space=pltpu.VMEM)
    shape = (chunks, 2, 2 * window, window)
    return pl.pallas_call(
        body,
        out_shape=(
            jax.ShapeDtypeStruct((1,) + shape, jnp.bfloat16),
            jax.ShapeDtypeStruct((2,) + shape, jnp.bfloat16),
        ),
        in_specs=[vmem] * 2,
        out_specs=(vmem, vmem),
        cost_estimate=cost(12 * width * width * size, 12 * width * width),
        name="dense_blocks",
    )(filter_in, filter_out)


def channel_mix(array, mats, conjugate):
    half = array.shape[0] // 2
    window = mats.shape[2]
    offset = window // 2
    parts = []
    for g in range(2):
        piece = array[:, g * offset : g * offset + window]
        re, im = piece[:half], piece[half:]
        if conjugate:
            rows = [jnp.concatenate([re, im], axis=1), jnp.concatenate([im, -re], axis=1)]
        else:
            rows = [jnp.concatenate([re, -im], axis=1), jnp.concatenate([im, re], axis=1)]
        parts.append(dot(jnp.concatenate(rows, axis=0), mats[g]))
    first, last = parts
    return jnp.concatenate(
        [first[:, :offset], first[:, offset:] + last[:, :offset], last[:, offset:]], axis=1
    )


def pack_outbox(obs_value, obs_weight, obs_index, block_dest, block_count, tiles):
    members, rows = obs_value.shape
    blocks = rows // OBS_BLK

    def body(dest_ref, count_ref, value_ref, weight_ref, index_ref, o_ref, seen_ref):
        o_ref[...] = jnp.zeros_like(o_ref)
        lane = lax.broadcasted_iota(jnp.int32, (1, OBS_BLK), 1)
        for t in range(tiles):
            seen_ref[t] = 0
        for b in range(blocks):
            tile = dest_ref[b]
            rank = seen_ref[tile]
            seen_ref[tile] = rank + 1
            span = slice(b * OBS_BLK, (b + 1) * OBS_BLK)
            weight = jnp.where(lane < count_ref[b], weight_ref[:, span], 0.0)
            o_ref[tile, pl.ds(pl.multiple_of(rank * members, members), members), :] = (
                value_ref[:, span] * weight
            )
            o_ref[tile, pl.ds(2 * members + rank, 1), :] = weight
            o_ref[tile, pl.ds(2 * members + 2 + rank, 1), :] = index_ref[:, span].astype(jnp.float32)

    smem = pl.BlockSpec(memory_space=pltpu.SMEM)
    vmem = pl.BlockSpec(memory_space=pltpu.VMEM)
    return pl.pallas_call(
        body,
        out_shape=jax.ShapeDtypeStruct((tiles, 2 * members + 8, OBS_BLK), jnp.float32),
        in_specs=[smem, smem, vmem, vmem, vmem],
        out_specs=vmem,
        scratch_shapes=[pltpu.SMEM((tiles,), jnp.int32)],
        name="pack_outbox",
    )(block_dest, block_count, obs_value, obs_weight, obs_index)


def regroup(arrays, pieces, rows):
    count = len(arrays)
    lead, height, lanes = arrays[0].shape
    shape = (count, height, lanes) if rows is None else (count, lead, rows, lanes)

    def body(*refs):
        for q in range(pieces):
            for r in range(count):
                if rows is None:
                    refs[count + q][r] = refs[r][q]
                else:
                    refs[count + q][r] = refs[r][:, q * rows : (q + 1) * rows]

    vmem = pl.BlockSpec(memory_space=pltpu.VMEM)
    return pl.pallas_call(
        body,
        out_shape=[jax.ShapeDtypeStruct(shape, arrays[0].dtype)] * pieces,
        in_specs=[vmem] * count,
        out_specs=[vmem] * pieces,
        name="regroup",
    )(*arrays)


def route(arrays, near, far):
    members = len(arrays)

    def shift(array, by_near, by_far):
        perm = [
            (z * near + y, (z + by_far) % far * near + (y + by_near) % near)
            for z in range(far)
            for y in range(near)
        ]
        return lax.ppermute(array, "space", perm)

    def ahead(array, by):
        return lax.ppermute(array, "lead", [(l, (l + by) % members) for l in range(members)])

    arrays = [arrays[0]] + [ahead(arrays[d], d) for d in range(1, members)]
    arrays = regroup(arrays, near, None)
    arrays = [arrays[0]] + [shift(arrays[r], r, 0) for r in range(1, near)]
    arrays = regroup(arrays, far, arrays[0].shape[1] // far)
    moved = [arrays[0]]
    for q in range(1, far):
        with jax.named_scope("far_%d" % q):
            moved.append(shift(arrays[q], 0, q))
    return moved


def level_spectra(received, decoded, matrix, here, near):
    sources, _, lanes = received.shape
    group = 4
    members, cells, levels = decoded.shape
    wide = 2 * lanes
    span = group * wide

    def body(here_ref, got_ref, dec_ref, mat_ref, *rest):
        o_refs, (cell_ref, val_ref, acc_ref) = rest[:members], rest[members:]
        acc_ref[...] = jnp.zeros_like(acc_ref)
        cell_iota = lax.broadcasted_iota(jnp.int32, (cells, wide), 0)
        level_iota = lax.broadcasted_iota(jnp.int32, (levels, wide), 0)

        def one_group(g, carry):
            for u in range(group):
                got = got_ref[g * group + u]
                index = jnp.concatenate(
                    [got[2 * members + 2 : 2 * members + 3], got[2 * members + 3 : 2 * members + 4]], axis=1
                ).astype(jnp.int32)
                cell, level = index // levels, index % levels
                first, second = u * wide, span + u * wide
                hot_cell = (cell_iota == cell).astype(jnp.bfloat16)
                cell_ref[:, first : first + wide] = hot_cell
                cell_ref[:, second : second + wide] = hot_cell
                hot_level = (level_iota == level).astype(jnp.bfloat16)
                weight = jnp.concatenate(
                    [got[2 * members : 2 * members + 1], got[2 * members + 1 : 2 * members + 2]], axis=1
                )
                value = jnp.concatenate([got[:members], got[members : 2 * members]], axis=1)
                full = jnp.concatenate([weight, value], axis=0)
                high = full.astype(jnp.bfloat16)
                low = (full - high.astype(jnp.float32)).astype(jnp.bfloat16)
                for q in range(members + 1):
                    at = slice(q * levels, (q + 1) * levels)
                    val_ref[at, first : first + wide] = hot_level * high[q : q + 1]
                    val_ref[at, second : second + wide] = hot_level * low[q : q + 1]
            acc_ref[...] += dot_nt(cell_ref[...], val_ref[...])
            return carry

        lax.fori_loop(0, sources // group, one_group, 0)
        weights = acc_ref[:, :levels]
        for ahead in range(members):
            member = (here_ref[0] + ahead) % members
            at = pl.multiple_of((member + 1) * levels, levels)
            forcing = weights * dec_ref[member] - acc_ref[:, pl.ds(at, levels)]
            spectrum = dot(mat_ref[...], forcing.astype(jnp.bfloat16)).astype(jnp.bfloat16)
            for r in range(near):
                o_refs[ahead][r] = spectrum[r * part : (r + 1) * part]

    part = matrix.shape[0] // near
    vmem = pl.BlockSpec(memory_space=pltpu.VMEM)
    return pl.pallas_call(
        body,
        out_shape=[jax.ShapeDtypeStruct((near, part, levels), jnp.bfloat16)] * members,
        in_specs=[pl.BlockSpec(memory_space=pltpu.SMEM)] + [vmem] * 3,
        out_specs=[vmem] * members,
        scratch_shapes=[
            pltpu.VMEM((cells, 2 * span), jnp.bfloat16),
            pltpu.VMEM(((members + 1) * levels, 2 * span), jnp.bfloat16),
            pltpu.VMEM((cells, (members + 1) * levels), jnp.float32),
        ],
        cost_estimate=cost(16 * sources * wide * cells * levels, 4 * members * cells * levels),
        name="level_spectra",
    )(here, received, decoded, matrix)


def slopes(spectra, merid, mats, bias, per_step=2):
    sections, rows, cols = spectra.shape
    chunks = mats.shape[1]
    width = cols // chunks
    half = rows // 2

    def body(x_ref, d_ref, w_ref, b_ref, o_ref):
        todo = [(u, c, slice(c * width, (c + 1) * width)) for u in range(per_step) for c in range(chunks)]
        modes = [dot(d_ref[...], x_ref[u, :, at]).astype(jnp.bfloat16) for u, c, at in todo]
        pres = [channel_mix(mode, w_ref[0, c], False) for mode, (u, c, at) in zip(modes, todo)]
        for pre, (u, c, at) in zip(pres, todo):
            o_ref[u, :half, at] = gelu_slope(pre[:half] + b_ref[0:1, at])
            o_ref[u, half:, at] = gelu_slope(pre[half:] + b_ref[1:2, at])

    part = pl.BlockSpec((per_step, rows, cols), lambda t: (t, 0, 0))
    return pl.pallas_call(
        body,
        out_shape=jax.ShapeDtypeStruct(spectra.shape, jnp.float32),
        grid=(sections // per_step,),
        in_specs=[
            part,
            pl.BlockSpec(merid.shape, lambda t: (0, 0)),
            pl.BlockSpec(mats.shape, lambda t: (0,) * mats.ndim),
            pl.BlockSpec(bias.shape, lambda t: (0, 0)),
        ],
        out_specs=part,
        cost_estimate=cost(3 * sections * rows * cols * width, 6 * sections * rows * cols),
        name="slopes",
    )(spectra, merid, mats, bias)


def sweep(slope, level_spec, merid, merid_t, mats, decoder, here, group, per_step=2):
    sections, rows, cols = slope.shape
    chunks = mats.shape[1]
    width = cols // chunks
    levels = decoder.shape[1]
    half = rows // 2
    lanes = 128
    far, (near, _, height, _) = len(level_spec), level_spec[0].shape
    steps = sections // per_step

    def body(here_ref, x_ref, d_ref, dt_ref, w_ref, dec_ref, *rest):
        f_refs, (o_ref, z_ref, f_ref, h_ref) = rest[:far], rest[far:]

        @pl.when(pl.program_id(0) == 0)
        def _():
            z_ref[...] = jnp.zeros_like(z_ref)
            for q in range(far):
                for r in range(near):
                    at = (q * near + r) * height
                    f_ref[:, at : at + height] = f_refs[q][r]
            row = lax.broadcasted_iota(jnp.int32, (rows, lanes), 0)
            zero = (row // group % (half // group) == 0) & (here_ref[1] == 0)
            paired = row % (group // 2) != 0
            real = row < half
            own = jnp.where(paired, 0.5, jnp.where(real, 1.0, 0.0))
            h_ref[0] = jnp.where(zero, own, 1.0)
            h_ref[1] = jnp.where(zero & paired, jnp.where(real, 0.5, -0.5), 0.0)

        keep = jnp.concatenate([h_ref[0]] * (width // lanes), axis=1)
        take = jnp.concatenate([h_ref[1]] * (width // lanes), axis=1)

        def hermitian(array):
            parts = []
            for g in range(0, rows, group):
                parts += [array[g + group // 2 : g + group], array[g : g + group // 2]]
            return keep * array + take * jnp.concatenate(parts, axis=0)

        spans = [slice(c * width, (c + 1) * width) for c in range(chunks)]
        carry = [z_ref[:, at] for at in spans]
        for u in reversed(range(per_step)):
            section = (steps - 1 - pl.program_id(0)) * per_step + u
            back = (here_ref[0] + sections - section) % sections
            forced = dot(d_ref[...], f_ref[back]).astype(jnp.bfloat16)
            hids = [
                channel_mix(hermitian(z).astype(jnp.bfloat16), w_ref[0, c], True)
                for c, z in enumerate(carry)
            ]
            pushed = [z + dot_nt(forced, dec_ref[at]) for z, at in zip(carry, spans)]
            acts = [(hid * x_ref[u, :, at]).astype(jnp.bfloat16) for hid, at in zip(hids, spans)]
            grads = [channel_mix(act, w_ref[1, c], True) for c, act in enumerate(acts)]
            carry = [push + hermitian(grad) for push, grad in zip(pushed, grads)]
            for z, at in zip(carry, spans):
                z_ref[:, at] = z
                o_ref[u, :, at] = dot(dt_ref[...], z.astype(jnp.bfloat16)).astype(jnp.bfloat16)

    turn = pl.BlockSpec((per_step, rows, cols), lambda t: (steps - 1 - t, 0, 0))
    square = pl.BlockSpec((rows, rows), lambda t: (0, 0))
    return pl.pallas_call(
        body,
        out_shape=jax.ShapeDtypeStruct((sections, rows, cols), jnp.bfloat16),
        grid=(steps,),
        in_specs=[
            pl.BlockSpec(memory_space=pltpu.SMEM),
            turn,
            square,
            square,
            pl.BlockSpec(mats.shape, lambda t: (0,) * mats.ndim),
            pl.BlockSpec((cols, levels), lambda t: (0, 0)),
        ]
        + [pl.BlockSpec(level_spec[0].shape, lambda t: (0, 0, 0, 0))] * far,
        out_specs=turn,
        scratch_shapes=[
            pltpu.VMEM((rows, cols), jnp.float32),
            pltpu.VMEM((sections, rows, levels), jnp.bfloat16),
            pltpu.VMEM((2, rows, lanes), jnp.float32),
        ],
        cost_estimate=cost(6 * sections * rows * cols * width, 6 * sections * rows * cols),
        name="sweep",
    )(here, slope, merid, merid_t, mats, decoder, *level_spec)


def swap(array, axis):
    batch, rows, cols = array.shape
    return lax.all_to_all(
        array.reshape(-1, 8, cols), axis, split_axis=0, concat_axis=0, tiled=True
    ).reshape(batch, rows, cols)


def shards(
    states,
    filter_in,
    filter_out,
    filter_bias,
    decoder,
    obs_value,
    obs_weight,
    obs_index,
    block_dest,
    block_count,
):
    member_count, lat_local, lon_len, channels = states.shape[1:]
    tiles = lax.axis_size("space")
    tables = {
        name: jnp.asarray(table, jnp.bfloat16)
        for name, table in make_matrices(tiles, lat_local, lon_len).items()
    }
    fields = states.reshape(member_count, lat_local * lon_len, channels)
    near = math.gcd(tiles, 4)
    far = tiles // near
    lead = lax.axis_index("lead").astype(jnp.int32)[None]
    tile = lax.axis_index("space").astype(jnp.int32)
    row = jnp.arange(tables["force"].shape[0], dtype=jnp.int32)
    high = row.shape[0] // tiles
    step_near, step_far = row // (far * high), row // high % far
    source = (tile // near + step_far) % far * near + (tile % near + step_near) % near
    picked = (source * high + row % high)[:, None] == row[None, :]
    force = dot(picked.astype(jnp.bfloat16), tables["force"]).astype(jnp.bfloat16)
    step_far, step_near = row // (near * high), row // high % near
    source = (tile // near + far - step_far) % far * near + (tile % near + near - step_near) % near
    picked = row[:, None] == (source * high + row % high)[None, :]
    merid = dot(tables["merid"], picked.astype(jnp.bfloat16)).astype(jnp.bfloat16)

    outbox = pack_outbox(obs_value[0], obs_weight, obs_index, block_dest[0], block_count[0], tiles)
    received = lax.all_to_all(outbox, "space", split_axis=0, concat_axis=0, tiled=True)
    mixed = mix_rows(tables["state"], fields)
    decoded = jnp.einsum("mnc,cv->mnv", fields, decoder, preferred_element_type=jnp.float32)
    mixed, received, decoded, force = lax.optimization_barrier((mixed, received, decoded, force))
    spectra = swap(mixed, EVERY)
    levels = route(level_spectra(received, decoded, force, lead, near), near, far)
    forward, adjoint = dense_blocks(filter_in, filter_out, 2)
    slope = slopes(spectra, tables["merid"], forward, filter_bias)
    here = jnp.concatenate([lead, tile[None]])
    swept = sweep(
        slope, levels, merid, tables["merid_t"], adjoint, decoder, here, tiles * lat_local
    )
    result = mix_rows(tables["back"], swap(swept, EVERY))
    return result.reshape(1, member_count, lat_local, lon_len, channels)


def solution(mesh):
    placed = (
        P("lead", None, "space", None, None),
        P(),
        P(),
        P(),
        P(),
        P("lead", None, "space"),
        P("lead", "space"),
        P("lead", "space"),
        P("lead", "space"),
        P("lead", "space"),
    )
    return jax.shard_map(
        shards,
        mesh=mesh,
        in_specs=placed,
        out_specs=P("lead", None, "space", None, None),
        check_vma=False,
    )
```

```python
import math

import jax
import jax.numpy as jnp
import numpy as np
from jax import lax
from jax.experimental import pallas as pl
from jax.experimental.pallas import tpu as pltpu
from jax.sharding import PartitionSpec as P

OBS_BLK = 128
EVERY = ("lead", "space")

root_scale = math.sqrt(2.0 / math.pi)
cubic_term = 0.044715


def gelu_slope(values):
    square = values * values
    tangent = jnp.tanh(values * (root_scale + (root_scale * cubic_term) * square))
    bend = values * ((0.5 * root_scale) + (1.5 * root_scale * cubic_term) * square)
    return 0.5 + 0.5 * tangent + bend * (1.0 - tangent * tangent)


def waves(rows, cols, length):
    angle = (np.outer(np.arange(rows), np.arange(cols)) % length) * (2.0 * math.pi / length)
    return np.cos(angle), np.sin(angle)


def make_matrices(tiles, lat_local, lon_len):
    lat_len, modes = tiles * lat_local, lon_len // 2
    pair = modes // tiles
    cos, sin = waves(modes, lon_len, lon_len)
    scale = 1.0 / math.sqrt(lon_len)
    gain = np.where(np.arange(modes) == 0, 1.0, 2.0)[:, None]
    nyquist = np.cos(math.pi * np.arange(lon_len)) * scale

    def zonal(factor, full):
        parts = np.stack([factor * cos * scale, -factor * sin * scale])
        parts[1, 0] = nyquist if full else 0.0
        parts = parts.reshape(2, tiles, pair, lon_len).transpose(1, 0, 2, 3)
        out = np.zeros((tiles, lat_local, 2, pair, lat_local, lon_len))
        for f in range(lat_local):
            out[:, f, :, :, f] = parts
        return out.reshape(tiles * lat_local * 2 * pair, lat_local * lon_len)

    lat_cos, lat_sin = (t / math.sqrt(lat_len) for t in waves(lat_len, lat_len, lat_len))
    merid = np.zeros((2, pair, lat_len, lat_len, 2, pair))
    for k in range(pair):
        merid[0, k, :, :, 0, k] = lat_cos
        merid[0, k, :, :, 1, k] = lat_sin
        merid[1, k, :, :, 0, k] = -lat_sin
        merid[1, k, :, :, 1, k] = lat_cos
    middle = lat_len // 2
    order = np.concatenate([np.arange(middle), [middle], np.arange(lat_len - 1, middle, -1)])
    merid = merid[:, :, order].reshape(2 * pair * lat_len, lat_len * 2 * pair)
    return {
        "state": zonal(1.0, False).astype(np.float32),
        "force": zonal(gain, True).astype(np.float32),
        "back": zonal(1.0, True).T.astype(np.float32),
        "merid": merid.astype(np.float32),
        "merid_t": merid.T.astype(np.float32),
    }


def dot(a, b):
    return lax.dot_general(a, b, (((1,), (0,)), ((), ())), preferred_element_type=jnp.float32)


def dot_nt(a, b):
    return lax.dot_general(a, b, (((1,), (1,)), ((), ())), preferred_element_type=jnp.float32)


def cost(products, moved):
    return pl.CostEstimate(flops=2 * products, transcendentals=0, bytes_accessed=moved)


def on_chip(array):
    return pltpu.with_memory_space_constraint(array, pltpu.VMEM)


def mix_rows(matrix, array, per_step=4, resident=False):
    batch, rows, cols = array.shape

    def body(m_ref, x_ref, o_ref):
        first = pl.program_id(0) * per_step if resident else 0
        for u in range(per_step):
            o_ref[u] = dot(m_ref[...], x_ref[first + u]).astype(jnp.bfloat16)

    part = pl.BlockSpec((per_step, rows, cols), lambda b: (b, 0, 0))
    return pl.pallas_call(
        body,
        out_shape=jax.ShapeDtypeStruct(array.shape, jnp.bfloat16),
        grid=(batch // per_step,),
        in_specs=[
            pl.BlockSpec((rows, rows), lambda b: (0, 0)),
            pl.BlockSpec(memory_space=pltpu.VMEM) if resident else part,
        ],
        out_specs=part,
        cost_estimate=cost(batch * rows * rows * cols, 4 * batch * rows * cols),
        compiler_params=pltpu.CompilerParams(vmem_limit_bytes=32 << 20),
        name="mix_rows",
    )(matrix, on_chip(array) if resident else array)


def dense_blocks(filter_in, filter_out, chunks):
    _, blocks, size, _ = filter_in.shape
    per = blocks // chunks
    width = per * size
    window, offset = 2 * width // 3, width // 3

    def body(in_ref, out_ref, f_ref, a_ref):
        row = lax.broadcasted_iota(jnp.int32, (width, width), 0)
        col = lax.broadcasted_iota(jnp.int32, (width, width), 1)
        same = row // size == col // size
        masks = [
            (same & (row < width // 2)).astype(jnp.float32),
            (same & (row >= width // 2)).astype(jnp.float32),
        ]
        row = lax.broadcasted_iota(jnp.int32, (width, size), 0)
        col = lax.broadcasted_iota(jnp.int32, (width, size), 1)
        lift = (row % size == col).astype(jnp.bfloat16)
        for c in range(chunks):
            for q in range(2):
                w_in = in_ref[q, c * per : (c + 1) * per].reshape(width, size)
                w_out = out_ref[q, c * per : (c + 1) * per].reshape(width, size)
                spread = [dot_nt(w_in, lift), dot_nt(lift, w_out), dot_nt(lift, w_in)]
                targets = [f_ref.at[0], a_ref.at[0], a_ref.at[1]]
                for whole, target in zip(spread, targets):
                    for g in range(2):
                        at = slice(g * offset, g * offset + window)
                        target[c, g, q * window : (q + 1) * window] = (
                            (whole * masks[g])[at, at].astype(jnp.bfloat16)
                        )

    vmem = pl.BlockSpec(memory_space=pltpu.VMEM)
    shape = (chunks, 2, 2 * window, window)
    return pl.pallas_call(
        body,
        out_shape=(
            jax.ShapeDtypeStruct((1,) + shape, jnp.bfloat16),
            jax.ShapeDtypeStruct((2,) + shape, jnp.bfloat16),
        ),
        in_specs=[vmem] * 2,
        out_specs=(vmem, vmem),
        cost_estimate=cost(12 * width * width * size, 12 * width * width),
        compiler_params=pltpu.CompilerParams(vmem_limit_bytes=32 << 20),
        name="dense_blocks",
    )(filter_in, filter_out)


def channel_mix(array, mats, conjugate):
    half = array.shape[0] // 2
    window = mats.shape[2]
    offset = window // 2
    parts = []
    for g in range(2):
        piece = array[:, g * offset : g * offset + window]
        re, im = piece[:half], piece[half:]
        if conjugate:
            rows = [jnp.concatenate([re, im], axis=1), jnp.concatenate([im, -re], axis=1)]
        else:
            rows = [jnp.concatenate([re, -im], axis=1), jnp.concatenate([im, re], axis=1)]
        parts.append(dot(jnp.concatenate(rows, axis=0), mats[g]))
    first, last = parts
    return jnp.concatenate(
        [first[:, :offset], first[:, offset:] + last[:, :offset], last[:, offset:]], axis=1
    )


def pack_outbox(obs_value, obs_weight, obs_index, block_dest, block_count, tiles):
    members, rows = obs_value.shape
    blocks = rows // OBS_BLK

    def body(dest_ref, count_ref, value_ref, weight_ref, index_ref, o_ref, seen_ref):
        o_ref[...] = jnp.zeros_like(o_ref)
        lane = lax.broadcasted_iota(jnp.int32, (1, OBS_BLK), 1)
        for t in range(tiles):
            seen_ref[t] = 0
        for b in range(blocks):
            tile = dest_ref[b]
            rank = seen_ref[tile]
            seen_ref[tile] = rank + 1
            span = slice(b * OBS_BLK, (b + 1) * OBS_BLK)
            weight = jnp.where(lane < count_ref[b], weight_ref[:, span], 0.0)
            o_ref[tile, pl.ds(pl.multiple_of(rank * members, members), members), :] = (
                value_ref[:, span] * weight
            )
            o_ref[tile, pl.ds(2 * members + rank, 1), :] = weight
            o_ref[tile, pl.ds(2 * members + 2 + rank, 1), :] = index_ref[:, span].astype(jnp.float32)

    smem = pl.BlockSpec(memory_space=pltpu.SMEM)
    vmem = pl.BlockSpec(memory_space=pltpu.VMEM)
    return pl.pallas_call(
        body,
        out_shape=jax.ShapeDtypeStruct((tiles, 2 * members + 8, OBS_BLK), jnp.float32),
        in_specs=[smem, smem, vmem, vmem, vmem],
        out_specs=vmem,
        scratch_shapes=[pltpu.SMEM((tiles,), jnp.int32)],
        name="pack_outbox",
    )(block_dest, block_count, obs_value, obs_weight, obs_index)


def regroup(arrays, pieces, rows):
    count = len(arrays)
    lead, height, lanes = arrays[0].shape
    shape = (count, height, lanes) if rows is None else (count, lead, rows, lanes)

    def body(*refs):
        for q in range(pieces):
            for r in range(count):
                if rows is None:
                    refs[count + q][r] = refs[r][q]
                else:
                    refs[count + q][r] = refs[r][:, q * rows : (q + 1) * rows]

    vmem = pl.BlockSpec(memory_space=pltpu.VMEM)
    return pl.pallas_call(
        body,
        out_shape=[jax.ShapeDtypeStruct(shape, arrays[0].dtype)] * pieces,
        in_specs=[vmem] * count,
        out_specs=[vmem] * pieces,
        compiler_params=pltpu.CompilerParams(vmem_limit_bytes=32 << 20),
        name="regroup",
    )(*[on_chip(array) for array in arrays])


def route(arrays, near, far):
    members = len(arrays)

    def shift(array, by_near, by_far):
        perm = [
            (z * near + y, (z + by_far) % far * near + (y + by_near) % near)
            for z in range(far)
            for y in range(near)
        ]
        return lax.ppermute(array, "space", perm)

    def ahead(array, by):
        return lax.ppermute(array, "lead", [(l, (l + by) % members) for l in range(members)])

    arrays = [arrays[0]] + [ahead(arrays[d], d) for d in range(1, members)]
    arrays = regroup(arrays, near, None)
    arrays = [arrays[0]] + [shift(arrays[r], r, 0) for r in range(1, near)]
    arrays = regroup(arrays, far, arrays[0].shape[1] // far)
    moved = [arrays[0]]
    for q in range(1, far):
        with jax.named_scope("far_%d" % q):
            moved.append(shift(arrays[q], 0, q))
    return moved


def level_spectra(received, decoded, matrix, here, near):
    sources, _, lanes = received.shape
    group = 4
    members, cells, levels = decoded.shape
    wide = 2 * lanes
    span = group * wide

    def body(here_ref, got_ref, dec_ref, mat_ref, *rest):
        o_refs, (cell_ref, val_ref, acc_ref) = rest[:members], rest[members:]
        acc_ref[...] = jnp.zeros_like(acc_ref)
        cell_iota = lax.broadcasted_iota(jnp.int32, (cells, wide), 0)
        level_iota = lax.broadcasted_iota(jnp.int32, (levels, wide), 0)

        def one_group(g, carry):
            for u in range(group):
                got = got_ref[g * group + u]
                index = jnp.concatenate(
                    [got[2 * members + 2 : 2 * members + 3], got[2 * members + 3 : 2 * members + 4]], axis=1
                ).astype(jnp.int32)
                cell, level = index // levels, index % levels
                first, second = u * wide, span + u * wide
                hot_cell = (cell_iota == cell).astype(jnp.bfloat16)
                cell_ref[:, first : first + wide] = hot_cell
                cell_ref[:, second : second + wide] = hot_cell
                hot_level = (level_iota == level).astype(jnp.bfloat16)
                weight = jnp.concatenate(
                    [got[2 * members : 2 * members + 1], got[2 * members + 1 : 2 * members + 2]], axis=1
                )
                value = jnp.concatenate([got[:members], got[members : 2 * members]], axis=1)
                full = jnp.concatenate([weight, value], axis=0)
                high = full.astype(jnp.bfloat16)
                low = (full - high.astype(jnp.float32)).astype(jnp.bfloat16)
                for q in range(members + 1):
                    at = slice(q * levels, (q + 1) * levels)
                    val_ref[at, first : first + wide] = hot_level * high[q : q + 1]
                    val_ref[at, second : second + wide] = hot_level * low[q : q + 1]
            acc_ref[...] += dot_nt(cell_ref[...], val_ref[...])
            return carry

        lax.fori_loop(0, sources // group, one_group, 0)
        weights = acc_ref[:, :levels]
        for ahead in range(members):
            member = (here_ref[0] + ahead) % members
            at = pl.multiple_of((member + 1) * levels, levels)
            forcing = weights * dec_ref[member] - acc_ref[:, pl.ds(at, levels)]
            spectrum = dot(mat_ref[...], forcing.astype(jnp.bfloat16)).astype(jnp.bfloat16)
            for r in range(near):
                o_refs[ahead][r] = spectrum[r * part : (r + 1) * part]

    part = matrix.shape[0] // near
    vmem = pl.BlockSpec(memory_space=pltpu.VMEM)
    return pl.pallas_call(
        body,
        out_shape=[jax.ShapeDtypeStruct((near, part, levels), jnp.bfloat16)] * members,
        in_specs=[pl.BlockSpec(memory_space=pltpu.SMEM)] + [vmem] * 3,
        out_specs=[vmem] * members,
        scratch_shapes=[
            pltpu.VMEM((cells, 2 * span), jnp.bfloat16),
            pltpu.VMEM(((members + 1) * levels, 2 * span), jnp.bfloat16),
            pltpu.VMEM((cells, (members + 1) * levels), jnp.float32),
        ],
        cost_estimate=cost(16 * sources * wide * cells * levels, 4 * members * cells * levels),
        compiler_params=pltpu.CompilerParams(vmem_limit_bytes=32 << 20),
        name="level_spectra",
    )(here, on_chip(received), decoded, matrix)


def slopes(spectra, merid, mats, bias, per_step=2):
    sections, rows, cols = spectra.shape
    chunks = mats.shape[1]
    width = cols // chunks
    half = rows // 2

    def body(x_ref, d_ref, w_ref, b_ref, o_ref):
        first = pl.program_id(0) * per_step
        todo = [(u, c, slice(c * width, (c + 1) * width)) for u in range(per_step) for c in range(chunks)]
        modes = [dot(d_ref[...], x_ref[first + u, :, at]).astype(jnp.bfloat16) for u, c, at in todo]
        pres = [channel_mix(mode, w_ref[0, c], False) for mode, (u, c, at) in zip(modes, todo)]
        for pre, (u, c, at) in zip(pres, todo):
            o_ref[u, :half, at] = gelu_slope(pre[:half] + b_ref[0:1, at])
            o_ref[u, half:, at] = gelu_slope(pre[half:] + b_ref[1:2, at])

    part = pl.BlockSpec((per_step, rows, cols), lambda t: (t, 0, 0))
    return pl.pallas_call(
        body,
        out_shape=jax.ShapeDtypeStruct(spectra.shape, jnp.float32),
        grid=(sections // per_step,),
        in_specs=[
            pl.BlockSpec(memory_space=pltpu.VMEM),
            pl.BlockSpec(merid.shape, lambda t: (0, 0)),
            pl.BlockSpec(memory_space=pltpu.VMEM),
            pl.BlockSpec(bias.shape, lambda t: (0, 0)),
        ],
        out_specs=part,
        cost_estimate=cost(3 * sections * rows * cols * width, 6 * sections * rows * cols),
        compiler_params=pltpu.CompilerParams(vmem_limit_bytes=32 << 20),
        name="slopes",
    )(on_chip(spectra), merid, on_chip(mats), bias)


def sweep(slope, level_spec, merid, merid_t, mats, decoder, here, group, per_step=2):
    sections, rows, cols = slope.shape
    chunks = mats.shape[1]
    width = cols // chunks
    levels = decoder.shape[1]
    half = rows // 2
    lanes = 128
    far, (near, _, height, _) = len(level_spec), level_spec[0].shape
    steps = sections // per_step

    def body(here_ref, x_ref, d_ref, dt_ref, w_ref, dec_ref, *rest):
        f_refs, (o_ref, z_ref, f_ref, h_ref) = rest[:far], rest[far:]

        @pl.when(pl.program_id(0) == 0)
        def _():
            z_ref[...] = jnp.zeros_like(z_ref)
            for q in range(far):
                for r in range(near):
                    at = (q * near + r) * height
                    f_ref[:, at : at + height] = f_refs[q][r]
            row = lax.broadcasted_iota(jnp.int32, (rows, lanes), 0)
            zero = (row // group % (half // group) == 0) & (here_ref[1] == 0)
            paired = row % (group // 2) != 0
            real = row < half
            own = jnp.where(paired, 0.5, jnp.where(real, 1.0, 0.0))
            h_ref[0] = jnp.where(zero, own, 1.0)
            h_ref[1] = jnp.where(zero & paired, jnp.where(real, 0.5, -0.5), 0.0)

        keep = jnp.concatenate([h_ref[0]] * (width // lanes), axis=1)
        take = jnp.concatenate([h_ref[1]] * (width // lanes), axis=1)

        def hermitian(array):
            parts = []
            for g in range(0, rows, group):
                parts += [array[g + group // 2 : g + group], array[g : g + group // 2]]
            return keep * array + take * jnp.concatenate(parts, axis=0)

        spans = [slice(c * width, (c + 1) * width) for c in range(chunks)]
        carry = [z_ref[:, at] for at in spans]
        for u in reversed(range(per_step)):
            section = (steps - 1 - pl.program_id(0)) * per_step + u
            back = (here_ref[0] + sections - section) % sections
            forced = dot(d_ref[...], f_ref[back]).astype(jnp.bfloat16)
            hids = [
                channel_mix(hermitian(z).astype(jnp.bfloat16), w_ref[0, c], True)
                for c, z in enumerate(carry)
            ]
            pushed = [z + dot_nt(forced, dec_ref[at]) for z, at in zip(carry, spans)]
            acts = [(hid * x_ref[u, :, at]).astype(jnp.bfloat16) for hid, at in zip(hids, spans)]
            grads = [channel_mix(act, w_ref[1, c], True) for c, act in enumerate(acts)]
            carry = [push + hermitian(grad) for push, grad in zip(pushed, grads)]
            for z, at in zip(carry, spans):
                z_ref[:, at] = z
                o_ref[u, :, at] = dot(dt_ref[...], z.astype(jnp.bfloat16)).astype(jnp.bfloat16)

    turn = pl.BlockSpec((per_step, rows, cols), lambda t: (steps - 1 - t, 0, 0))
    square = pl.BlockSpec((rows, rows), lambda t: (0, 0))
    return pl.pallas_call(
        body,
        out_shape=jax.ShapeDtypeStruct((sections, rows, cols), jnp.bfloat16),
        grid=(steps,),
        in_specs=[
            pl.BlockSpec(memory_space=pltpu.SMEM),
            turn,
            square,
            square,
            pl.BlockSpec(memory_space=pltpu.VMEM),
            pl.BlockSpec((cols, levels), lambda t: (0, 0)),
        ]
        + [pl.BlockSpec(memory_space=pltpu.VMEM)] * far,
        out_specs=turn,
        scratch_shapes=[
            pltpu.VMEM((rows, cols), jnp.float32),
            pltpu.VMEM((sections, rows, levels), jnp.bfloat16),
            pltpu.VMEM((2, rows, lanes), jnp.float32),
        ],
        cost_estimate=cost(6 * sections * rows * cols * width, 6 * sections * rows * cols),
        compiler_params=pltpu.CompilerParams(vmem_limit_bytes=32 << 20),
        name="sweep",
    )(here, slope, merid, merid_t, on_chip(mats), decoder, *[on_chip(piece) for piece in level_spec])


def swap(array, axis):
    batch, rows, cols = array.shape
    return lax.all_to_all(
        array.reshape(-1, 8, cols), axis, split_axis=0, concat_axis=0, tiled=True
    ).reshape(batch, rows, cols)


def shards(
    states,
    filter_in,
    filter_out,
    filter_bias,
    decoder,
    obs_value,
    obs_weight,
    obs_index,
    block_dest,
    block_count,
):
    member_count, lat_local, lon_len, channels = states.shape[1:]
    tiles = lax.axis_size("space")
    tables = {
        name: jnp.asarray(table, jnp.bfloat16)
        for name, table in make_matrices(tiles, lat_local, lon_len).items()
    }
    fields = states.reshape(member_count, lat_local * lon_len, channels)
    near = math.gcd(tiles, 4)
    far = tiles // near
    lead = lax.axis_index("lead").astype(jnp.int32)[None]
    tile = lax.axis_index("space").astype(jnp.int32)
    row = jnp.arange(tables["force"].shape[0], dtype=jnp.int32)
    high = row.shape[0] // tiles
    step_near, step_far = row // (far * high), row // high % far
    source = (tile // near + step_far) % far * near + (tile % near + step_near) % near
    picked = (source * high + row % high)[:, None] == row[None, :]
    force = dot(picked.astype(jnp.bfloat16), tables["force"]).astype(jnp.bfloat16)
    step_far, step_near = row // (near * high), row // high % near
    source = (tile // near + far - step_far) % far * near + (tile % near + near - step_near) % near
    picked = row[:, None] == (source * high + row % high)[None, :]
    merid = dot(tables["merid"], picked.astype(jnp.bfloat16)).astype(jnp.bfloat16)

    outbox = pack_outbox(obs_value[0], obs_weight, obs_index, block_dest[0], block_count[0], tiles)
    received = lax.all_to_all(outbox, "space", split_axis=0, concat_axis=0, tiled=True)
    mixed = mix_rows(tables["state"], fields)
    decoded = jnp.einsum("mnc,cv->mnv", fields, decoder, preferred_element_type=jnp.float32)
    mixed, received, decoded, force = lax.optimization_barrier((mixed, received, decoded, force))
    spectra = swap(mixed, EVERY)
    levels = route(level_spectra(received, decoded, force, lead, near), near, far)
    forward, adjoint = dense_blocks(filter_in, filter_out, 2)
    slope = slopes(spectra, tables["merid"], forward, filter_bias)
    here = jnp.concatenate([lead, tile[None]])
    swept = sweep(
        slope, levels, merid, tables["merid_t"], adjoint, decoder, here, tiles * lat_local
    )
    result = mix_rows(tables["back"], swap(swept, EVERY), resident=True)
    return result.reshape(1, member_count, lat_local, lon_len, channels)


def solution(mesh):
    placed = (
        P("lead", None, "space", None, None),
        P(),
        P(),
        P(),
        P(),
        P("lead", None, "space"),
        P("lead", "space"),
        P("lead", "space"),
        P("lead", "space"),
        P("lead", "space"),
    )
    return jax.shard_map(
        shards,
        mesh=mesh,
        in_specs=placed,
        out_specs=P("lead", None, "space", None, None),
        check_vma=False,
    )
```

```python
import math

import jax
import jax.numpy as jnp
import numpy as np
from jax import lax
from jax.experimental import pallas as pl
from jax.experimental.pallas import tpu as pltpu
from jax.sharding import PartitionSpec as P

OBS_BLK = 128
EVERY = ("lead", "space")

root_scale = math.sqrt(2.0 / math.pi)
cubic_term = 0.044715


def gelu_slope(values):
    square = values * values
    tangent = jnp.tanh(values * (root_scale + (root_scale * cubic_term) * square))
    bend = values * ((0.5 * root_scale) + (1.5 * root_scale * cubic_term) * square)
    return 0.5 + 0.5 * tangent + bend * (1.0 - tangent * tangent)


def waves(rows, cols, length):
    angle = (np.outer(np.arange(rows), np.arange(cols)) % length) * (2.0 * math.pi / length)
    return np.cos(angle), np.sin(angle)


def make_matrices(tiles, lat_local, lon_len):
    lat_len, modes = tiles * lat_local, lon_len // 2
    pair = modes // tiles
    cos, sin = waves(modes, lon_len, lon_len)
    scale = 1.0 / math.sqrt(lon_len)
    gain = np.where(np.arange(modes) == 0, 1.0, 2.0)[:, None]
    nyquist = np.cos(math.pi * np.arange(lon_len)) * scale

    def zonal(factor, full):
        parts = np.stack([factor * cos * scale, -factor * sin * scale])
        parts[1, 0] = nyquist if full else 0.0
        parts = parts.reshape(2, tiles, pair, lon_len).transpose(1, 0, 2, 3)
        out = np.zeros((tiles, lat_local, 2, pair, lat_local, lon_len))
        for f in range(lat_local):
            out[:, f, :, :, f] = parts
        return out.reshape(tiles * lat_local * 2 * pair, lat_local * lon_len)

    lat_cos, lat_sin = (t / math.sqrt(lat_len) for t in waves(lat_len, lat_len, lat_len))
    merid = np.zeros((2, pair, lat_len, lat_len, 2, pair))
    for k in range(pair):
        merid[0, k, :, :, 0, k] = lat_cos
        merid[0, k, :, :, 1, k] = lat_sin
        merid[1, k, :, :, 0, k] = -lat_sin
        merid[1, k, :, :, 1, k] = lat_cos
    middle = lat_len // 2
    order = np.concatenate([np.arange(middle), [middle], np.arange(lat_len - 1, middle, -1)])
    merid = merid[:, :, order].reshape(2 * pair * lat_len, lat_len * 2 * pair)
    return {
        "state": zonal(1.0, False).astype(np.float32),
        "force": zonal(gain, True).astype(np.float32),
        "back": zonal(1.0, True).T.astype(np.float32),
        "merid": merid.astype(np.float32),
        "merid_t": merid.T.astype(np.float32),
    }


def dot(a, b):
    return lax.dot_general(a, b, (((1,), (0,)), ((), ())), preferred_element_type=jnp.float32)


def dot_nt(a, b):
    return lax.dot_general(a, b, (((1,), (1,)), ((), ())), preferred_element_type=jnp.float32)


def cost(products, moved):
    return pl.CostEstimate(flops=2 * products, transcendentals=0, bytes_accessed=moved)


def on_chip(array):
    return pltpu.with_memory_space_constraint(array, pltpu.VMEM)


def mix_rows(matrix, array, per_step=4, resident=False):
    batch, rows, cols = array.shape

    def body(m_ref, x_ref, o_ref):
        first = pl.program_id(0) * per_step if resident else 0
        for u in range(per_step):
            o_ref[u] = dot(m_ref[...], x_ref[first + u]).astype(jnp.bfloat16)

    part = pl.BlockSpec((per_step, rows, cols), lambda b: (b, 0, 0))
    return pl.pallas_call(
        body,
        out_shape=jax.ShapeDtypeStruct(array.shape, jnp.bfloat16),
        grid=(batch // per_step,),
        in_specs=[
            pl.BlockSpec((rows, rows), lambda b: (0, 0)),
            pl.BlockSpec(memory_space=pltpu.VMEM) if resident else part,
        ],
        out_specs=part,
        cost_estimate=cost(batch * rows * rows * cols, 4 * batch * rows * cols),
        compiler_params=pltpu.CompilerParams(vmem_limit_bytes=32 << 20),
        name="mix_rows",
    )(matrix, on_chip(array) if resident else array)


def dense_blocks(filter_in, filter_out, chunks):
    _, blocks, size, _ = filter_in.shape
    per = blocks // chunks
    width = per * size
    window, offset = 2 * width // 3, width // 3

    def body(in_ref, out_ref, f_ref, a_ref):
        row = lax.broadcasted_iota(jnp.int32, (width, width), 0)
        col = lax.broadcasted_iota(jnp.int32, (width, width), 1)
        same = row // size == col // size
        masks = [
            (same & (row < width // 2)).astype(jnp.float32),
            (same & (row >= width // 2)).astype(jnp.float32),
        ]
        row = lax.broadcasted_iota(jnp.int32, (width, size), 0)
        col = lax.broadcasted_iota(jnp.int32, (width, size), 1)
        lift = (row % size == col).astype(jnp.bfloat16)
        for c in range(chunks):
            for q in range(2):
                w_in = in_ref[q, c * per : (c + 1) * per].reshape(width, size)
                w_out = out_ref[q, c * per : (c + 1) * per].reshape(width, size)
                spread = [dot_nt(w_in, lift), dot_nt(lift, w_out), dot_nt(lift, w_in)]
                targets = [f_ref.at[0], a_ref.at[0], a_ref.at[1]]
                for whole, target in zip(spread, targets):
                    for g in range(2):
                        at = slice(g * offset, g * offset + window)
                        target[c, g, q * window : (q + 1) * window] = (
                            (whole * masks[g])[at, at].astype(jnp.bfloat16)
                        )

    vmem = pl.BlockSpec(memory_space=pltpu.VMEM)
    shape = (chunks, 2, 2 * window, window)
    return pl.pallas_call(
        body,
        out_shape=(
            jax.ShapeDtypeStruct((1,) + shape, jnp.bfloat16),
            jax.ShapeDtypeStruct((2,) + shape, jnp.bfloat16),
        ),
        in_specs=[vmem] * 2,
        out_specs=(vmem, vmem),
        cost_estimate=cost(12 * width * width * size, 12 * width * width),
        compiler_params=pltpu.CompilerParams(vmem_limit_bytes=32 << 20),
        name="dense_blocks",
    )(filter_in, filter_out)


def channel_mix(array, mats, conjugate):
    half = array.shape[0] // 2
    window = mats.shape[2]
    offset = window // 2
    parts = []
    for g in range(2):
        piece = array[:, g * offset : g * offset + window]
        re, im = piece[:half], piece[half:]
        if conjugate:
            rows = [jnp.concatenate([re, im], axis=1), jnp.concatenate([im, -re], axis=1)]
        else:
            rows = [jnp.concatenate([re, -im], axis=1), jnp.concatenate([im, re], axis=1)]
        parts.append(dot(jnp.concatenate(rows, axis=0), mats[g]))
    first, last = parts
    return jnp.concatenate(
        [first[:, :offset], first[:, offset:] + last[:, :offset], last[:, offset:]], axis=1
    )


def pack_outbox(obs_value, obs_weight, obs_index, block_dest, block_count, tiles):
    members, rows = obs_value.shape
    blocks = rows // OBS_BLK

    def body(dest_ref, count_ref, value_ref, weight_ref, index_ref, o_ref, seen_ref):
        o_ref[...] = jnp.zeros_like(o_ref)
        lane = lax.broadcasted_iota(jnp.int32, (1, OBS_BLK), 1)
        for t in range(tiles):
            seen_ref[t] = 0
        for b in range(blocks):
            tile = dest_ref[b]
            rank = seen_ref[tile]
            seen_ref[tile] = rank + 1
            span = slice(b * OBS_BLK, (b + 1) * OBS_BLK)
            weight = jnp.where(lane < count_ref[b], weight_ref[:, span], 0.0)
            o_ref[tile, pl.ds(pl.multiple_of(rank * members, members), members), :] = (
                value_ref[:, span] * weight
            )
            o_ref[tile, pl.ds(2 * members + rank, 1), :] = weight
            o_ref[tile, pl.ds(2 * members + 2 + rank, 1), :] = index_ref[:, span].astype(jnp.float32)

    smem = pl.BlockSpec(memory_space=pltpu.SMEM)
    vmem = pl.BlockSpec(memory_space=pltpu.VMEM)
    return pl.pallas_call(
        body,
        out_shape=jax.ShapeDtypeStruct((tiles, 2 * members + 8, OBS_BLK), jnp.float32),
        in_specs=[smem, smem, vmem, vmem, vmem],
        out_specs=vmem,
        scratch_shapes=[pltpu.SMEM((tiles,), jnp.int32)],
        name="pack_outbox",
    )(block_dest, block_count, obs_value, obs_weight, obs_index)


def regroup(arrays, pieces, rows):
    count = len(arrays)
    lead, height, lanes = arrays[0].shape
    shape = (count, height, lanes) if rows is None else (count, lead, rows, lanes)

    def body(*refs):
        for q in range(pieces):
            for r in range(count):
                if rows is None:
                    refs[count + q][r] = refs[r][q]
                else:
                    refs[count + q][r] = refs[r][:, q * rows : (q + 1) * rows]

    vmem = pl.BlockSpec(memory_space=pltpu.VMEM)
    return pl.pallas_call(
        body,
        out_shape=[jax.ShapeDtypeStruct(shape, arrays[0].dtype)] * pieces,
        in_specs=[vmem] * count,
        out_specs=[vmem] * pieces,
        compiler_params=pltpu.CompilerParams(vmem_limit_bytes=32 << 20),
        name="regroup",
    )(*[on_chip(array) for array in arrays])


def route(arrays, near, far):
    members = len(arrays)

    def shift(array, by_near, by_far):
        perm = [
            (z * near + y, (z + by_far) % far * near + (y + by_near) % near)
            for z in range(far)
            for y in range(near)
        ]
        return lax.ppermute(array, "space", perm)

    def ahead(array, by):
        return lax.ppermute(array, "lead", [(l, (l + by) % members) for l in range(members)])

    arrays = [arrays[0]] + [ahead(arrays[d], d) for d in range(1, members)]
    arrays = regroup(arrays, near, None)
    arrays = [arrays[0]] + [shift(arrays[r], r, 0) for r in range(1, near)]
    arrays = regroup(arrays, far, arrays[0].shape[1] // far)
    moved = [arrays[0]]
    for q in range(1, far):
        with jax.named_scope("far_%d" % q):
            moved.append(shift(arrays[q], 0, q))
    return moved


def level_spectra(received, decoded, matrix, here, near):
    sources, _, lanes = received.shape
    group = 4
    members, cells, levels = decoded.shape
    wide = 2 * lanes
    span = group * wide

    def body(here_ref, got_ref, dec_ref, mat_ref, *rest):
        o_refs, (cell_ref, val_ref, acc_ref) = rest[:members], rest[members:]
        acc_ref[...] = jnp.zeros_like(acc_ref)
        cell_iota = lax.broadcasted_iota(jnp.int32, (cells, wide), 0)
        level_iota = lax.broadcasted_iota(jnp.int32, (levels, wide), 0)

        def one_group(g, carry):
            for u in range(group):
                got = got_ref[g * group + u]
                index = jnp.concatenate(
                    [got[2 * members + 2 : 2 * members + 3], got[2 * members + 3 : 2 * members + 4]], axis=1
                ).astype(jnp.int32)
                cell, level = index // levels, index % levels
                first, second = u * wide, span + u * wide
                hot_cell = (cell_iota == cell).astype(jnp.bfloat16)
                cell_ref[:, first : first + wide] = hot_cell
                cell_ref[:, second : second + wide] = hot_cell
                hot_level = (level_iota == level).astype(jnp.bfloat16)
                weight = jnp.concatenate(
                    [got[2 * members : 2 * members + 1], got[2 * members + 1 : 2 * members + 2]], axis=1
                )
                value = jnp.concatenate([got[:members], got[members : 2 * members]], axis=1)
                full = jnp.concatenate([weight, value], axis=0)
                high = full.astype(jnp.bfloat16)
                low = (full - high.astype(jnp.float32)).astype(jnp.bfloat16)
                for q in range(members + 1):
                    at = slice(q * levels, (q + 1) * levels)
                    val_ref[at, first : first + wide] = hot_level * high[q : q + 1]
                    val_ref[at, second : second + wide] = hot_level * low[q : q + 1]
            acc_ref[...] += dot_nt(cell_ref[...], val_ref[...])
            return carry

        lax.fori_loop(0, sources // group, one_group, 0)
        weights = acc_ref[:, :levels]
        for ahead in range(members):
            member = (here_ref[0] + ahead) % members
            at = pl.multiple_of((member + 1) * levels, levels)
            forcing = weights * dec_ref[member] - acc_ref[:, pl.ds(at, levels)]
            spectrum = dot(mat_ref[...], forcing.astype(jnp.bfloat16)).astype(jnp.bfloat16)
            for r in range(near):
                o_refs[ahead][r] = spectrum[r * part : (r + 1) * part]

    part = matrix.shape[0] // near
    vmem = pl.BlockSpec(memory_space=pltpu.VMEM)
    return pl.pallas_call(
        body,
        out_shape=[jax.ShapeDtypeStruct((near, part, levels), jnp.bfloat16)] * members,
        in_specs=[pl.BlockSpec(memory_space=pltpu.SMEM)] + [vmem] * 3,
        out_specs=[vmem] * members,
        scratch_shapes=[
            pltpu.VMEM((cells, 2 * span), jnp.bfloat16),
            pltpu.VMEM(((members + 1) * levels, 2 * span), jnp.bfloat16),
            pltpu.VMEM((cells, (members + 1) * levels), jnp.float32),
        ],
        cost_estimate=cost(16 * sources * wide * cells * levels, 4 * members * cells * levels),
        compiler_params=pltpu.CompilerParams(vmem_limit_bytes=32 << 20),
        name="level_spectra",
    )(here, on_chip(received), decoded, matrix)


def slopes(spectra, merid, mats, bias, per_step=4):
    sections, rows, cols = spectra.shape
    chunks = mats.shape[1]
    width = cols // chunks
    half = rows // 2

    def body(x_ref, d_ref, w_ref, b_ref, o_ref):
        first = pl.program_id(0) * per_step
        todo = [(u, c, slice(c * width, (c + 1) * width)) for u in range(per_step) for c in range(chunks)]
        modes = [dot(d_ref[...], x_ref[first + u, :, at]).astype(jnp.bfloat16) for u, c, at in todo]
        pres = [channel_mix(mode, w_ref[0, c], False) for mode, (u, c, at) in zip(modes, todo)]
        for pre, (u, c, at) in zip(pres, todo):
            o_ref[u, :half, at] = gelu_slope(pre[:half] + b_ref[0:1, at])
            o_ref[u, half:, at] = gelu_slope(pre[half:] + b_ref[1:2, at])

    part = pl.BlockSpec((per_step, rows, cols), lambda t: (t, 0, 0))
    return pl.pallas_call(
        body,
        out_shape=jax.ShapeDtypeStruct(spectra.shape, jnp.float32),
        grid=(sections // per_step,),
        in_specs=[
            pl.BlockSpec(memory_space=pltpu.VMEM),
            pl.BlockSpec(merid.shape, lambda t: (0, 0)),
            pl.BlockSpec(memory_space=pltpu.VMEM),
            pl.BlockSpec(bias.shape, lambda t: (0, 0)),
        ],
        out_specs=part,
        cost_estimate=cost(3 * sections * rows * cols * width, 6 * sections * rows * cols),
        compiler_params=pltpu.CompilerParams(vmem_limit_bytes=32 << 20),
        name="slopes",
    )(on_chip(spectra), merid, on_chip(mats), bias)


def sweep(slope, level_spec, merid, merid_t, mats, decoder, here, group, per_step=8):
    sections, rows, cols = slope.shape
    chunks = mats.shape[1]
    width = cols // chunks
    levels = decoder.shape[1]
    half = rows // 2
    lanes = 128
    far, (near, _, height, _) = len(level_spec), level_spec[0].shape
    steps = sections // per_step

    def body(here_ref, x_ref, d_ref, dt_ref, w_ref, dec_ref, *rest):
        f_refs, (o_ref, z_ref, f_ref, h_ref) = rest[:far], rest[far:]

        @pl.when(pl.program_id(0) == 0)
        def _():
            z_ref[...] = jnp.zeros_like(z_ref)
            for q in range(far):
                for r in range(near):
                    at = (q * near + r) * height
                    f_ref[:, at : at + height] = f_refs[q][r]
            row = lax.broadcasted_iota(jnp.int32, (rows, lanes), 0)
            zero = (row // group % (half // group) == 0) & (here_ref[1] == 0)
            paired = row % (group // 2) != 0
            real = row < half
            own = jnp.where(paired, 0.5, jnp.where(real, 1.0, 0.0))
            h_ref[0] = jnp.where(zero, own, 1.0)
            h_ref[1] = jnp.where(zero & paired, jnp.where(real, 0.5, -0.5), 0.0)

        keep = jnp.concatenate([h_ref[0]] * (width // lanes), axis=1)
        take = jnp.concatenate([h_ref[1]] * (width // lanes), axis=1)

        def hermitian(array):
            parts = []
            for g in range(0, rows, group):
                parts += [array[g + group // 2 : g + group], array[g : g + group // 2]]
            return keep * array + take * jnp.concatenate(parts, axis=0)

        spans = [slice(c * width, (c + 1) * width) for c in range(chunks)]
        carry = [z_ref[:, at] for at in spans]
        for u in reversed(range(per_step)):
            section = (steps - 1 - pl.program_id(0)) * per_step + u
            back = (here_ref[0] + sections - section) % sections
            forced = dot(d_ref[...], f_ref[back]).astype(jnp.bfloat16)
            hids = [
                channel_mix(hermitian(z).astype(jnp.bfloat16), w_ref[0, c], True)
                for c, z in enumerate(carry)
            ]
            pushed = [z + dot_nt(forced, dec_ref[at]) for z, at in zip(carry, spans)]
            acts = [(hid * x_ref[u, :, at]).astype(jnp.bfloat16) for hid, at in zip(hids, spans)]
            grads = [channel_mix(act, w_ref[1, c], True) for c, act in enumerate(acts)]
            carry = [push + hermitian(grad) for push, grad in zip(pushed, grads)]
            for z, at in zip(carry, spans):
                z_ref[:, at] = z
                o_ref[u, :, at] = dot(dt_ref[...], z.astype(jnp.bfloat16)).astype(jnp.bfloat16)

    turn = pl.BlockSpec((per_step, rows, cols), lambda t: (steps - 1 - t, 0, 0))
    square = pl.BlockSpec((rows, rows), lambda t: (0, 0))
    return pl.pallas_call(
        body,
        out_shape=jax.ShapeDtypeStruct((sections, rows, cols), jnp.bfloat16),
        grid=(steps,),
        in_specs=[
            pl.BlockSpec(memory_space=pltpu.SMEM),
            turn,
            square,
            square,
            pl.BlockSpec(memory_space=pltpu.VMEM),
            pl.BlockSpec((cols, levels), lambda t: (0, 0)),
        ]
        + [pl.BlockSpec(memory_space=pltpu.VMEM)] * far,
        out_specs=turn,
        scratch_shapes=[
            pltpu.VMEM((rows, cols), jnp.float32),
            pltpu.VMEM((sections, rows, levels), jnp.bfloat16),
            pltpu.VMEM((2, rows, lanes), jnp.float32),
        ],
        cost_estimate=cost(6 * sections * rows * cols * width, 6 * sections * rows * cols),
        compiler_params=pltpu.CompilerParams(vmem_limit_bytes=32 << 20),
        name="sweep",
    )(here, slope, merid, merid_t, on_chip(mats), decoder, *[on_chip(piece) for piece in level_spec])


def swap(array, axis):
    batch, rows, cols = array.shape
    return lax.all_to_all(
        array.reshape(-1, 8, cols), axis, split_axis=0, concat_axis=0, tiled=True
    ).reshape(batch, rows, cols)


def shards(
    states,
    filter_in,
    filter_out,
    filter_bias,
    decoder,
    obs_value,
    obs_weight,
    obs_index,
    block_dest,
    block_count,
):
    member_count, lat_local, lon_len, channels = states.shape[1:]
    tiles = lax.axis_size("space")
    tables = {
        name: jnp.asarray(table, jnp.bfloat16)
        for name, table in make_matrices(tiles, lat_local, lon_len).items()
    }
    fields = states.reshape(member_count, lat_local * lon_len, channels)
    near = math.gcd(tiles, 4)
    far = tiles // near
    lead = lax.axis_index("lead").astype(jnp.int32)[None]
    tile = lax.axis_index("space").astype(jnp.int32)
    row = jnp.arange(tables["force"].shape[0], dtype=jnp.int32)
    high = row.shape[0] // tiles
    step_near, step_far = row // (far * high), row // high % far
    source = (tile // near + step_far) % far * near + (tile % near + step_near) % near
    picked = (source * high + row % high)[:, None] == row[None, :]
    force = dot(picked.astype(jnp.bfloat16), tables["force"]).astype(jnp.bfloat16)
    step_far, step_near = row // (near * high), row // high % near
    source = (tile // near + far - step_far) % far * near + (tile % near + near - step_near) % near
    picked = row[:, None] == (source * high + row % high)[None, :]
    merid = dot(tables["merid"], picked.astype(jnp.bfloat16)).astype(jnp.bfloat16)

    outbox = pack_outbox(obs_value[0], obs_weight, obs_index, block_dest[0], block_count[0], tiles)
    received = lax.all_to_all(outbox, "space", split_axis=0, concat_axis=0, tiled=True)
    mixed = mix_rows(tables["state"], fields)
    decoded = jnp.einsum("mnc,cv->mnv", fields, decoder, preferred_element_type=jnp.float32)
    mixed, received, decoded, force = lax.optimization_barrier((mixed, received, decoded, force))
    spectra = swap(mixed, EVERY)
    levels = route(level_spectra(received, decoded, force, lead, near), near, far)
    forward, adjoint = dense_blocks(filter_in, filter_out, 2)
    slope = slopes(spectra, tables["merid"], forward, filter_bias)
    here = jnp.concatenate([lead, tile[None]])
    swept = sweep(
        slope, levels, merid, tables["merid_t"], adjoint, decoder, here, tiles * lat_local
    )
    result = mix_rows(tables["back"], swap(swept, EVERY), resident=True)
    return result.reshape(1, member_count, lat_local, lon_len, channels)


def solution(mesh):
    placed = (
        P("lead", None, "space", None, None),
        P(),
        P(),
        P(),
        P(),
        P("lead", None, "space"),
        P("lead", "space"),
        P("lead", "space"),
        P("lead", "space"),
        P("lead", "space"),
    )
    return jax.shard_map(
        shards,
        mesh=mesh,
        in_specs=placed,
        out_specs=P("lead", None, "space", None, None),
        check_vma=False,
    )
```

```python
import math

import jax
import jax.numpy as jnp
import numpy as np
from jax import lax
from jax.experimental import pallas as pl
from jax.experimental.pallas import tpu as pltpu
from jax.sharding import PartitionSpec as P

OBS_BLK = 128
EVERY = ("lead", "space")

root_scale = math.sqrt(2.0 / math.pi)
cubic_term = 0.044715


def gelu_slope(values):
    square = values * values
    tangent = jnp.tanh(values * (root_scale + (root_scale * cubic_term) * square))
    bend = values * ((0.5 * root_scale) + (1.5 * root_scale * cubic_term) * square)
    return 0.5 + 0.5 * tangent + bend * (1.0 - tangent * tangent)


def waves(rows, cols, length):
    angle = (np.outer(np.arange(rows), np.arange(cols)) % length) * (2.0 * math.pi / length)
    return np.cos(angle), np.sin(angle)


def make_matrices(tiles, lat_local, lon_len):
    lat_len, modes = tiles * lat_local, lon_len // 2
    pair = modes // tiles
    cos, sin = waves(modes, lon_len, lon_len)
    scale = 1.0 / math.sqrt(lon_len)
    gain = np.where(np.arange(modes) == 0, 1.0, 2.0)[:, None]
    nyquist = np.cos(math.pi * np.arange(lon_len)) * scale

    def zonal(factor, full):
        parts = np.stack([factor * cos * scale, -factor * sin * scale])
        parts[1, 0] = nyquist if full else 0.0
        parts = parts.reshape(2, tiles, pair, lon_len).transpose(1, 0, 2, 3)
        out = np.zeros((tiles, lat_local, 2, pair, lat_local, lon_len))
        for f in range(lat_local):
            out[:, f, :, :, f] = parts
        return out.reshape(tiles * lat_local * 2 * pair, lat_local * lon_len)

    lat_cos, lat_sin = (t / math.sqrt(lat_len) for t in waves(lat_len, lat_len, lat_len))
    merid = np.zeros((2, pair, lat_len, lat_len, 2, pair))
    for k in range(pair):
        merid[0, k, :, :, 0, k] = lat_cos
        merid[0, k, :, :, 1, k] = lat_sin
        merid[1, k, :, :, 0, k] = -lat_sin
        merid[1, k, :, :, 1, k] = lat_cos
    middle = lat_len // 2
    order = np.concatenate([np.arange(middle), [middle], np.arange(lat_len - 1, middle, -1)])
    merid = merid[:, :, order].reshape(2 * pair * lat_len, lat_len * 2 * pair)
    return {
        "state": zonal(1.0, False).astype(np.float32),
        "force": zonal(gain, True).astype(np.float32),
        "back": zonal(1.0, True).T.astype(np.float32),
        "merid": merid.astype(np.float32),
        "merid_t": merid.T.astype(np.float32),
    }


def dot(a, b):
    return lax.dot_general(a, b, (((1,), (0,)), ((), ())), preferred_element_type=jnp.float32)


def dot_nt(a, b):
    return lax.dot_general(a, b, (((1,), (1,)), ((), ())), preferred_element_type=jnp.float32)


def cost(products, moved):
    return pl.CostEstimate(flops=2 * products, transcendentals=0, bytes_accessed=moved)


def on_chip(array):
    return pltpu.with_memory_space_constraint(array, pltpu.VMEM)


def mix_rows(matrix, array, per_step=4, resident=False):
    batch, rows, cols = array.shape

    def body(m_ref, x_ref, o_ref):
        first = pl.program_id(0) * per_step if resident else 0
        for u in range(per_step):
            o_ref[u] = dot(m_ref[...], x_ref[first + u]).astype(jnp.bfloat16)

    part = pl.BlockSpec((per_step, rows, cols), lambda b: (b, 0, 0))
    return pl.pallas_call(
        body,
        out_shape=jax.ShapeDtypeStruct(array.shape, jnp.bfloat16),
        grid=(batch // per_step,),
        in_specs=[
            pl.BlockSpec((rows, rows), lambda b: (0, 0)),
            pl.BlockSpec(memory_space=pltpu.VMEM) if resident else part,
        ],
        out_specs=part,
        cost_estimate=cost(batch * rows * rows * cols, 4 * batch * rows * cols),
        compiler_params=pltpu.CompilerParams(vmem_limit_bytes=32 << 20),
        name="mix_rows",
    )(matrix, on_chip(array) if resident else array)


def dense_blocks(filter_in, filter_out, chunks):
    _, blocks, size, _ = filter_in.shape
    per = blocks // chunks
    width = per * size
    window, offset = 2 * width // 3, width // 3

    def body(in_ref, out_ref, f_ref, a_ref):
        row = lax.broadcasted_iota(jnp.int32, (width, width), 0)
        col = lax.broadcasted_iota(jnp.int32, (width, width), 1)
        same = row // size == col // size
        masks = [
            (same & (row < width // 2)).astype(jnp.float32),
            (same & (row >= width // 2)).astype(jnp.float32),
        ]
        row = lax.broadcasted_iota(jnp.int32, (width, size), 0)
        col = lax.broadcasted_iota(jnp.int32, (width, size), 1)
        lift = (row % size == col).astype(jnp.bfloat16)
        for c in range(chunks):
            for q in range(2):
                w_in = in_ref[q, c * per : (c + 1) * per].reshape(width, size)
                w_out = out_ref[q, c * per : (c + 1) * per].reshape(width, size)
                spread = [dot_nt(w_in, lift), dot_nt(lift, w_out), dot_nt(lift, w_in)]
                targets = [f_ref.at[0], a_ref.at[0], a_ref.at[1]]
                for whole, target in zip(spread, targets):
                    for g in range(2):
                        at = slice(g * offset, g * offset + window)
                        target[c, g, q * window : (q + 1) * window] = (
                            (whole * masks[g])[at, at].astype(jnp.bfloat16)
                        )

    vmem = pl.BlockSpec(memory_space=pltpu.VMEM)
    shape = (chunks, 2, 2 * window, window)
    return pl.pallas_call(
        body,
        out_shape=(
            jax.ShapeDtypeStruct((1,) + shape, jnp.bfloat16),
            jax.ShapeDtypeStruct((2,) + shape, jnp.bfloat16),
        ),
        in_specs=[vmem] * 2,
        out_specs=(vmem, vmem),
        cost_estimate=cost(12 * width * width * size, 12 * width * width),
        compiler_params=pltpu.CompilerParams(vmem_limit_bytes=32 << 20),
        name="dense_blocks",
    )(filter_in, filter_out)


def channel_mix(array, mats, conjugate):
    half = array.shape[0] // 2
    window = mats.shape[2]
    offset = window // 2
    parts = []
    for g in range(2):
        piece = array[:, g * offset : g * offset + window]
        re, im = piece[:half], piece[half:]
        if conjugate:
            rows = [jnp.concatenate([re, im], axis=1), jnp.concatenate([im, -re], axis=1)]
        else:
            rows = [jnp.concatenate([re, -im], axis=1), jnp.concatenate([im, re], axis=1)]
        parts.append(dot(jnp.concatenate(rows, axis=0), mats[g]))
    first, last = parts
    return jnp.concatenate(
        [first[:, :offset], first[:, offset:] + last[:, :offset], last[:, offset:]], axis=1
    )


def pack_outbox(obs_value, obs_weight, obs_index, block_dest, block_count, tiles):
    members, rows = obs_value.shape
    blocks = rows // OBS_BLK

    def body(dest_ref, count_ref, value_ref, weight_ref, index_ref, o_ref, seen_ref):
        o_ref[...] = jnp.zeros_like(o_ref)
        lane = lax.broadcasted_iota(jnp.int32, (1, OBS_BLK), 1)
        for t in range(tiles):
            seen_ref[t] = 0
        for b in range(blocks):
            tile = dest_ref[b]
            rank = seen_ref[tile]
            seen_ref[tile] = rank + 1
            span = slice(b * OBS_BLK, (b + 1) * OBS_BLK)
            weight = jnp.where(lane < count_ref[b], weight_ref[:, span], 0.0)
            o_ref[tile, pl.ds(pl.multiple_of(rank * members, members), members), :] = (
                value_ref[:, span] * weight
            )
            o_ref[tile, pl.ds(2 * members + rank, 1), :] = weight
            o_ref[tile, pl.ds(2 * members + 2 + rank, 1), :] = index_ref[:, span].astype(jnp.float32)

    smem = pl.BlockSpec(memory_space=pltpu.SMEM)
    vmem = pl.BlockSpec(memory_space=pltpu.VMEM)
    return pl.pallas_call(
        body,
        out_shape=jax.ShapeDtypeStruct((tiles, 2 * members + 8, OBS_BLK), jnp.float32),
        in_specs=[smem, smem, vmem, vmem, vmem],
        out_specs=vmem,
        scratch_shapes=[pltpu.SMEM((tiles,), jnp.int32)],
        compiler_params=pltpu.CompilerParams(vmem_limit_bytes=32 << 20),
        name="pack_outbox",
    )(block_dest, block_count, obs_value, obs_weight, obs_index)


def regroup(arrays, pieces, rows):
    count = len(arrays)
    lead, height, lanes = arrays[0].shape
    shape = (count, height, lanes) if rows is None else (count, lead, rows, lanes)

    def body(*refs):
        for q in range(pieces):
            for r in range(count):
                if rows is None:
                    refs[count + q][r] = refs[r][q]
                else:
                    refs[count + q][r] = refs[r][:, q * rows : (q + 1) * rows]

    vmem = pl.BlockSpec(memory_space=pltpu.VMEM)
    return pl.pallas_call(
        body,
        out_shape=[jax.ShapeDtypeStruct(shape, arrays[0].dtype)] * pieces,
        in_specs=[vmem] * count,
        out_specs=[vmem] * pieces,
        compiler_params=pltpu.CompilerParams(vmem_limit_bytes=32 << 20),
        name="regroup",
    )(*[on_chip(array) for array in arrays])


def route(arrays, near, far):
    members = len(arrays)

    def shift(array, by_near, by_far):
        perm = [
            (z * near + y, (z + by_far) % far * near + (y + by_near) % near)
            for z in range(far)
            for y in range(near)
        ]
        return lax.ppermute(array, "space", perm)

    def ahead(array, by):
        return lax.ppermute(array, "lead", [(l, (l + by) % members) for l in range(members)])

    arrays = [arrays[0]] + [ahead(arrays[d], d) for d in range(1, members)]
    arrays = regroup(arrays, near, None)
    arrays = [arrays[0]] + [shift(arrays[r], r, 0) for r in range(1, near)]
    arrays = regroup(arrays, far, arrays[0].shape[1] // far)
    moved = [arrays[0]]
    for q in range(1, far):
        with jax.named_scope("far_%d" % q):
            moved.append(shift(arrays[q], 0, q))
    return moved


def level_spectra(received, decoded, matrix, here, near):
    sources, _, lanes = received.shape
    group = 4
    members, cells, levels = decoded.shape
    wide = 2 * lanes
    span = group * wide

    def body(here_ref, got_ref, dec_ref, mat_ref, *rest):
        o_refs, (cell_ref, val_ref, acc_ref) = rest[:members], rest[members:]
        acc_ref[...] = jnp.zeros_like(acc_ref)
        cell_iota = lax.broadcasted_iota(jnp.int32, (cells, wide), 0)
        level_iota = lax.broadcasted_iota(jnp.int32, (levels, wide), 0)

        def one_group(g, carry):
            for u in range(group):
                got = got_ref[g * group + u]
                index = jnp.concatenate(
                    [got[2 * members + 2 : 2 * members + 3], got[2 * members + 3 : 2 * members + 4]], axis=1
                ).astype(jnp.int32)
                cell, level = index // levels, index % levels
                first, second = u * wide, span + u * wide
                hot_cell = (cell_iota == cell).astype(jnp.bfloat16)
                cell_ref[:, first : first + wide] = hot_cell
                cell_ref[:, second : second + wide] = hot_cell
                hot_level = (level_iota == level).astype(jnp.bfloat16)
                weight = jnp.concatenate(
                    [got[2 * members : 2 * members + 1], got[2 * members + 1 : 2 * members + 2]], axis=1
                )
                value = jnp.concatenate([got[:members], got[members : 2 * members]], axis=1)
                full = jnp.concatenate([weight, value], axis=0)
                high = full.astype(jnp.bfloat16)
                low = (full - high.astype(jnp.float32)).astype(jnp.bfloat16)
                for q in range(members + 1):
                    at = slice(q * levels, (q + 1) * levels)
                    val_ref[at, first : first + wide] = hot_level * high[q : q + 1]
                    val_ref[at, second : second + wide] = hot_level * low[q : q + 1]
            acc_ref[...] += dot_nt(cell_ref[...], val_ref[...])
            return carry

        lax.fori_loop(0, sources // group, one_group, 0)
        weights = acc_ref[:, :levels]
        for ahead in range(members):
            member = (here_ref[0] + ahead) % members
            at = pl.multiple_of((member + 1) * levels, levels)
            forcing = weights * dec_ref[member] - acc_ref[:, pl.ds(at, levels)]
            spectrum = dot(mat_ref[...], forcing.astype(jnp.bfloat16)).astype(jnp.bfloat16)
            for r in range(near):
                o_refs[ahead][r] = spectrum[r * part : (r + 1) * part]

    part = matrix.shape[0] // near
    vmem = pl.BlockSpec(memory_space=pltpu.VMEM)
    return pl.pallas_call(
        body,
        out_shape=[jax.ShapeDtypeStruct((near, part, levels), jnp.bfloat16)] * members,
        in_specs=[pl.BlockSpec(memory_space=pltpu.SMEM)] + [vmem] * 3,
        out_specs=[vmem] * members,
        scratch_shapes=[
            pltpu.VMEM((cells, 2 * span), jnp.bfloat16),
            pltpu.VMEM(((members + 1) * levels, 2 * span), jnp.bfloat16),
            pltpu.VMEM((cells, (members + 1) * levels), jnp.float32),
        ],
        cost_estimate=cost(16 * sources * wide * cells * levels, 4 * members * cells * levels),
        compiler_params=pltpu.CompilerParams(vmem_limit_bytes=32 << 20),
        name="level_spectra",
    )(here, on_chip(received), decoded, matrix)


def slopes(spectra, merid, mats, bias, per_step=4):
    sections, rows, cols = spectra.shape
    chunks = mats.shape[1]
    width = cols // chunks
    half = rows // 2

    def body(x_ref, d_ref, w_ref, b_ref, o_ref):
        first = pl.program_id(0) * per_step
        todo = [(u, c, slice(c * width, (c + 1) * width)) for u in range(per_step) for c in range(chunks)]
        modes = [dot(d_ref[...], x_ref[first + u, :, at]).astype(jnp.bfloat16) for u, c, at in todo]
        pres = [channel_mix(mode, w_ref[0, c], False) for mode, (u, c, at) in zip(modes, todo)]
        for pre, (u, c, at) in zip(pres, todo):
            o_ref[u, :half, at] = gelu_slope(pre[:half] + b_ref[0:1, at])
            o_ref[u, half:, at] = gelu_slope(pre[half:] + b_ref[1:2, at])

    part = pl.BlockSpec((per_step, rows, cols), lambda t: (t, 0, 0))
    return pl.pallas_call(
        body,
        out_shape=jax.ShapeDtypeStruct(spectra.shape, jnp.float32),
        grid=(sections // per_step,),
        in_specs=[
            pl.BlockSpec(memory_space=pltpu.VMEM),
            pl.BlockSpec(merid.shape, lambda t: (0, 0)),
            pl.BlockSpec(memory_space=pltpu.VMEM),
            pl.BlockSpec(bias.shape, lambda t: (0, 0)),
        ],
        out_specs=part,
        cost_estimate=cost(3 * sections * rows * cols * width, 6 * sections * rows * cols),
        compiler_params=pltpu.CompilerParams(vmem_limit_bytes=32 << 20),
        name="slopes",
    )(on_chip(spectra), merid, on_chip(mats), bias)


def sweep(slope, level_spec, merid, merid_t, mats, decoder, here, group, per_step=8):
    sections, rows, cols = slope.shape
    chunks = mats.shape[1]
    width = cols // chunks
    levels = decoder.shape[1]
    half = rows // 2
    lanes = 128
    far, (near, _, height, _) = len(level_spec), level_spec[0].shape
    steps = sections // per_step

    def body(here_ref, x_ref, d_ref, dt_ref, w_ref, dec_ref, *rest):
        f_refs, (o_ref, z_ref, f_ref, h_ref) = rest[:far], rest[far:]

        @pl.when(pl.program_id(0) == 0)
        def _():
            z_ref[...] = jnp.zeros_like(z_ref)
            for q in range(far):
                for r in range(near):
                    at = (q * near + r) * height
                    f_ref[:, at : at + height] = f_refs[q][r]
            row = lax.broadcasted_iota(jnp.int32, (rows, lanes), 0)
            zero = (row // group % (half // group) == 0) & (here_ref[1] == 0)
            paired = row % (group // 2) != 0
            real = row < half
            own = jnp.where(paired, 0.5, jnp.where(real, 1.0, 0.0))
            h_ref[0] = jnp.where(zero, own, 1.0)
            h_ref[1] = jnp.where(zero & paired, jnp.where(real, 0.5, -0.5), 0.0)

        keep = jnp.concatenate([h_ref[0]] * (width // lanes), axis=1)
        take = jnp.concatenate([h_ref[1]] * (width // lanes), axis=1)

        def hermitian(array):
            parts = []
            for g in range(0, rows, group):
                parts += [array[g + group // 2 : g + group], array[g : g + group // 2]]
            return keep * array + take * jnp.concatenate(parts, axis=0)

        spans = [slice(c * width, (c + 1) * width) for c in range(chunks)]
        carry = [z_ref[:, at] for at in spans]
        for u in reversed(range(per_step)):
            section = (steps - 1 - pl.program_id(0)) * per_step + u
            back = (here_ref[0] + sections - section) % sections
            forced = dot(d_ref[...], f_ref[back]).astype(jnp.bfloat16)
            hids = [
                channel_mix(hermitian(z).astype(jnp.bfloat16), w_ref[0, c], True)
                for c, z in enumerate(carry)
            ]
            pushed = [z + dot_nt(forced, dec_ref[at]) for z, at in zip(carry, spans)]
            acts = [(hid * x_ref[u, :, at]).astype(jnp.bfloat16) for hid, at in zip(hids, spans)]
            grads = [channel_mix(act, w_ref[1, c], True) for c, act in enumerate(acts)]
            carry = [push + hermitian(grad) for push, grad in zip(pushed, grads)]
            for z, at in zip(carry, spans):
                z_ref[:, at] = z
                o_ref[u, :, at] = dot(dt_ref[...], z.astype(jnp.bfloat16)).astype(jnp.bfloat16)

    turn = pl.BlockSpec((per_step, rows, cols), lambda t: (steps - 1 - t, 0, 0))
    square = pl.BlockSpec((rows, rows), lambda t: (0, 0))
    return pl.pallas_call(
        body,
        out_shape=jax.ShapeDtypeStruct((sections, rows, cols), jnp.bfloat16),
        grid=(steps,),
        in_specs=[
            pl.BlockSpec(memory_space=pltpu.SMEM),
            turn,
            square,
            square,
            pl.BlockSpec(memory_space=pltpu.VMEM),
            pl.BlockSpec((cols, levels), lambda t: (0, 0)),
        ]
        + [pl.BlockSpec(memory_space=pltpu.VMEM)] * far,
        out_specs=turn,
        scratch_shapes=[
            pltpu.VMEM((rows, cols), jnp.float32),
            pltpu.VMEM((sections, rows, levels), jnp.bfloat16),
            pltpu.VMEM((2, rows, lanes), jnp.float32),
        ],
        cost_estimate=cost(6 * sections * rows * cols * width, 6 * sections * rows * cols),
        compiler_params=pltpu.CompilerParams(vmem_limit_bytes=32 << 20),
        name="sweep",
    )(here, slope, merid, merid_t, on_chip(mats), decoder, *[on_chip(piece) for piece in level_spec])


def swap(array, axis):
    batch, rows, cols = array.shape
    return lax.all_to_all(
        array.reshape(-1, 8, cols), axis, split_axis=0, concat_axis=0, tiled=True
    ).reshape(batch, rows, cols)


def shards(
    states,
    filter_in,
    filter_out,
    filter_bias,
    decoder,
    obs_value,
    obs_weight,
    obs_index,
    block_dest,
    block_count,
):
    member_count, lat_local, lon_len, channels = states.shape[1:]
    tiles = lax.axis_size("space")
    tables = {
        name: jnp.asarray(table, jnp.bfloat16)
        for name, table in make_matrices(tiles, lat_local, lon_len).items()
    }
    fields = states.reshape(member_count, lat_local * lon_len, channels)
    near = math.gcd(tiles, 4)
    far = tiles // near
    lead = lax.axis_index("lead").astype(jnp.int32)[None]
    tile = lax.axis_index("space").astype(jnp.int32)
    row = jnp.arange(tables["force"].shape[0], dtype=jnp.int32)
    high = row.shape[0] // tiles
    step_near, step_far = row // (far * high), row // high % far
    source = (tile // near + step_far) % far * near + (tile % near + step_near) % near
    picked = (source * high + row % high)[:, None] == row[None, :]
    force = dot(picked.astype(jnp.bfloat16), tables["force"]).astype(jnp.bfloat16)
    step_far, step_near = row // (near * high), row // high % near
    source = (tile // near + far - step_far) % far * near + (tile % near + near - step_near) % near
    picked = row[:, None] == (source * high + row % high)[None, :]
    merid = dot(tables["merid"], picked.astype(jnp.bfloat16)).astype(jnp.bfloat16)

    outbox = pack_outbox(obs_value[0], obs_weight, obs_index, block_dest[0], block_count[0], tiles)
    received = lax.all_to_all(outbox, "space", split_axis=0, concat_axis=0, tiled=True)
    mixed = mix_rows(tables["state"], fields)
    decoded = jnp.einsum("mnc,cv->mnv", fields, decoder, preferred_element_type=jnp.float32)
    mixed, received, decoded, force = lax.optimization_barrier((mixed, received, decoded, force))
    spectra = swap(mixed, EVERY)
    levels = route(level_spectra(received, decoded, force, lead, near), near, far)
    forward, adjoint = dense_blocks(filter_in, filter_out, 2)
    slope = slopes(spectra, tables["merid"], forward, filter_bias)
    here = jnp.concatenate([lead, tile[None]])
    swept = sweep(
        slope, levels, merid, tables["merid_t"], adjoint, decoder, here, tiles * lat_local
    )
    result = mix_rows(tables["back"], swap(swept, EVERY), resident=True)
    return result.reshape(1, member_count, lat_local, lon_len, channels)


def solution(mesh):
    placed = (
        P("lead", None, "space", None, None),
        P(),
        P(),
        P(),
        P(),
        P("lead", None, "space"),
        P("lead", "space"),
        P("lead", "space"),
        P("lead", "space"),
        P("lead", "space"),
    )
    return jax.shard_map(
        shards,
        mesh=mesh,
        in_specs=placed,
        out_specs=P("lead", None, "space", None, None),
        check_vma=False,
    )
```
